32 devices in a mesh: seq: 2 (over x), shard: 4 (over y, core), rep: 4 (over z).
Axes of the slice: x: 2, y: 2, z: 4, core: 2. Of those that a mesh axis runs over, the one named last changes fastest.
Arguments:
- tokens: bfloat16 [32, 1024, 768], P(('shard', 'rep'), 'seq'), may hold values from -6 to 6
- segment_ids: int32 [32, 1024], P(('shard', 'rep')), may hold values from 0 to 17, as said below
- out_grad: bfloat16 [32, 1024, 768], P(('shard', 'rep'), 'seq'), may hold values from -6 to 6
- norm1_gain: bfloat16 [768], P('shard'), may hold values from 0.5 to 1.5
- norm1_bias: bfloat16 [768], P('shard'), may hold values from -1.75 to 1.75
- qkv_weight: bfloat16 [768, 2304], P('shard'), may hold values from -0.21875 to 0.21875
- query_bias: bfloat16 [768], P('shard'), may hold values from -3 to 3
- value_bias: bfloat16 [768], P('shard'), may hold values from -3 to 3
- out_weight: bfloat16 [768, 768], P('shard'), may hold values from -0.625 to 0.625
- out_bias: bfloat16 [768], P('shard'), may hold values from -1.75 to 1.75
- norm2_gain: bfloat16 [768], P('shard'), may hold values from 0.5 to 1.5
- norm2_bias: bfloat16 [768], P('shard'), may hold values from -1.75 to 1.75
- ff_in_weight: bfloat16 [768, 3072], P('shard'), may hold values from -0.21875 to 0.21875
- ff_in_bias: bfloat16 [3072], P('shard'), may hold values from -3 to 3
- ff_out_weight: bfloat16 [3072, 768], P('shard'), may hold values from -0.109375 to 0.109375
- ff_out_bias: bfloat16 [768], P('shard'), may hold values from -1.75 to 1.75
Outputs:
- block_out: bfloat16 [32, 1024, 768], P(('shard', 'rep'), 'seq')
- tokens_grad: bfloat16 [32, 1024, 768], P(('shard', 'rep'), 'seq')
- norm1_gain_grad: float32 [768], P('shard')
- norm1_bias_grad: float32 [768], P('shard')
- qkv_weight_grad: float32 [768, 2304], P('shard')
- query_bias_grad: float32 [768], P('shard')
- value_bias_grad: float32 [768], P('shard')
- out_weight_grad: float32 [768, 768], P('shard')
- out_bias_grad: float32 [768], P('shard')
- norm2_gain_grad: float32 [768], P('shard')
- norm2_bias_grad: float32 [768], P('shard')
- ff_in_weight_grad: float32 [768, 3072], P('shard')
- ff_in_bias_grad: float32 [3072], P('shard')
- ff_out_weight_grad: float32 [3072, 768], P('shard')
- ff_out_bias_grad: float32 [768], P('shard')
The draws below stay inside these ranges and needn't reach their ends.
Inputs may be any that keep to these rules, and one draw needn't show every extreme that they name: `segment_ids`: within each sequence the ids never fall; documents are numbered 1, 2, 3 and so on in order of position, each a run of 60 to 800 rows; 0 marks padding, which only follows the last document.
All inputs are finite; a program needn't handle non-finite values.
Results may differ from the reference program's by a relative error of at most 0.013.
The reference program's roundings to bfloat16 on the way count: a program that leaves them out, or rounds other values in their place, can miss the bound.
Values may be sent and summed in bfloat16 or wider, within the bound.
No kernel may reach another device: no remote copies, remote signals or barrier semaphores. Data moves between devices by JAX's collectives and lax.ppermute only.
A program may use at most 256 MiB of HBM per device.

```python
import jax
import jax.numpy as jnp
from jax import lax

D = 768
HEADS = 12
HEAD_DIM = 64
FF = 3072
DOC_MIN = 60
DOC_MAX = 800
SEQ_LEN = 1024
SEQS = 32


def draw_segment_ids(key, part):
    doc_count = SEQ_LEN // DOC_MIN + 1
    doc_lengths = jax.random.randint(key, (SEQS, doc_count), DOC_MIN, DOC_MAX + 1)
    seq_index = jnp.arange(SEQS, dtype=jnp.int32)[:, None]
    doc_lengths = jnp.where(seq_index == 0, DOC_MIN, doc_lengths)
    doc_lengths = jnp.where(seq_index == SEQS - 1, DOC_MAX, doc_lengths).astype(jnp.int32)
    doc_ends = jnp.cumsum(doc_lengths, axis=1)
    position = jnp.arange(SEQ_LEN, dtype=jnp.int32)[None, :, None]
    ends_wide = doc_ends[:, None, :]
    doc_index = jnp.sum((ends_wide <= position).astype(jnp.int32), axis=2)
    far_value = jnp.int32(2 * SEQ_LEN + DOC_MAX * doc_count)
    finish = jnp.min(jnp.where(ends_wide > position, ends_wide, far_value), axis=2)
    return jnp.where(finish <= SEQ_LEN, doc_index + 1, 0).astype(jnp.int32)


def block_levels(stream_key, extent, split, low, top_value):
    gain, own = 1.0, jax.random.fold_in(stream_key, 6)
    for dim, shards_of in split:
        heights = jnp.exp(jax.random.uniform(jax.random.fold_in(own, dim), (shards_of,), jnp.float32, low / len(split), top_value / len(split)))
        gain = gain * jnp.repeat(heights, extent[dim] // shards_of).reshape([-1 if axis == dim else 1 for axis in range(len(extent))])
    return gain


def noise(key, extent, deviation, most, cuts=(), kind=jnp.bfloat16):
    array = deviation * jax.random.normal(key, extent, jnp.float32)
    if cuts:
        array = array * block_levels(key, extent, cuts, -0.22, 0.18)
    return jnp.clip(array, -most, most).astype(kind)


def setup_inputs(seed: int = 0) -> dict:
    splits = jax.random.split(jax.random.key(seed), 17)
    return {
        "tokens": noise(splits[0], (SEQS, SEQ_LEN, D), 1.0, 6.0, ((0, 16), (1, 2))),
        "segment_ids": draw_segment_ids(jax.random.fold_in(splits[16], 71), 0),
        "out_grad": noise(splits[2], (SEQS, SEQ_LEN, D), 1.0, 6.0, ((0, 16), (1, 2))),
        "norm1_gain": jnp.clip(1.0 + 0.1 * jax.random.normal(splits[3], (D,), jnp.float32), 0.5, 1.5).astype(jnp.bfloat16),
        "norm1_bias": noise(splits[4], (D,), 0.3, 1.75, ((0, 4),)),
        "qkv_weight": noise(splits[5], (D, 3 * D), D ** -0.5, 0.21875, ((0, 4),)),
        "query_bias": noise(splits[6], (D,), 0.5, 3.0, ((0, 4),)),
        "value_bias": noise(splits[7], (D,), 0.5, 3.0, ((0, 4),)),
        "out_weight": noise(splits[8], (D, D), (D // 8) ** -0.5, 0.625, ((0, 4),)),
        "out_bias": noise(splits[9], (D,), 0.3, 1.75, ((0, 4),)),
        "norm2_gain": jnp.clip(1.0 + 0.1 * jax.random.normal(splits[10], (D,), jnp.float32), 0.5, 1.5).astype(jnp.bfloat16),
        "norm2_bias": noise(splits[11], (D,), 0.3, 1.75, ((0, 4),)),
        "ff_in_weight": noise(splits[12], (D, FF), D ** -0.5, 0.21875, ((0, 4),)),
        "ff_in_bias": noise(splits[13], (FF,), 0.5, 3.0, ((0, 4),)),
        "ff_out_weight": noise(splits[14], (FF, D), FF ** -0.5, 0.109375, ((0, 4),)),
        "ff_out_bias": noise(splits[15], (D,), 0.3, 1.75, ((0, 4),)),
    }


@jax.custom_vjp
def low(v):
    return lax.optimization_barrier(v.astype(jnp.bfloat16)).astype(jnp.float32)

@jax.custom_vjp
def low_back(v):
    return v

def low_keep(v):
    return (low(v), None)

def low_pass(kept, grad):
    return (grad,)

def back_keep(v):
    return (v, None)

def back_low(kept, grad):
    return (low(grad),)
low.defvjp(low_keep, low_pass)
low_back.defvjp(back_keep, back_low)

def norm_rows(inputs, gain_row, shift_row):
    row_mean = lax.optimization_barrier(jnp.mean(inputs, axis=-1, keepdims=True))
    centered = inputs - row_mean
    row_var = lax.optimization_barrier(jnp.mean(centered * centered, axis=-1, keepdims=True))
    return centered * lax.rsqrt(row_var + 1e-06) * gain_row + shift_row

def mat_high(left, right):
    return jnp.dot(left, right, precision=lax.Precision.HIGHEST, preferred_element_type=jnp.float32)

def one_sequence(weights, seq_tokens, seq_ids):
    n1_gain, n1_bias, w_qkv, q_bias, v_bias, w_out, o_bias, n2_gain, n2_bias, w_in, in_bias, w_back, back_bias = weights
    seq_rows = seq_tokens.shape[0]
    normed = low(norm_rows(seq_tokens, n1_gain, n1_bias))
    qkv_bias = jnp.concatenate([q_bias, jnp.zeros_like(q_bias), v_bias])
    qkv_all = low(low_back(mat_high(normed, w_qkv) + qkv_bias))
    queries = qkv_all[:, :D].reshape(seq_rows, HEADS, HEAD_DIM)
    keys_all = qkv_all[:, D:2 * D].reshape(seq_rows, HEADS, HEAD_DIM)
    values_all = qkv_all[:, 2 * D:].reshape(seq_rows, HEADS, HEAD_DIM)
    scores = jnp.einsum('qhd,khd->hqk', queries, keys_all, precision=lax.Precision.HIGHEST) * HEAD_DIM ** (-0.5)
    scores = low_back(scores)
    allowed = seq_ids[:, None] == seq_ids[None, :]
    scores = jnp.where(allowed[None], scores, -1e+30)
    probs = low(jax.nn.softmax(scores, axis=-1))
    mixed = jnp.einsum('hqk,khd->qhd', probs, values_all, precision=lax.Precision.HIGHEST).reshape(seq_rows, D)
    mixed = low(low_back(mixed))
    resid = seq_tokens + low_back(mat_high(mixed, w_out) + o_bias)
    hidden_in = low_back(mat_high(low(norm_rows(resid, n2_gain, n2_bias)), w_in) + in_bias)
    hidden = low(jax.nn.gelu(hidden_in, approximate=False))
    return resid + low_back(mat_high(hidden, w_back) + back_bias)

def reference(tokens, segment_ids, out_grad, norm1_gain, norm1_bias, qkv_weight, query_bias, value_bias, out_weight, out_bias, norm2_gain, norm2_bias, ff_in_weight, ff_in_bias, ff_out_weight, ff_out_bias):
    weights = tuple((entry.astype(jnp.float32) for entry in (norm1_gain, norm1_bias, qkv_weight, query_bias, value_bias, out_weight, out_bias, norm2_gain, norm2_bias, ff_in_weight, ff_in_bias, ff_out_weight, ff_out_bias)))
    inputs = tokens.astype(jnp.float32)
    seq_fn = jax.checkpoint(one_sequence)

    def whole_layer(weight_set, token_set):

        def per_seq(carry_val, seq_item):
            return (carry_val, seq_fn(weight_set, seq_item[0], seq_item[1]))
        _, result = lax.scan(per_seq, jnp.zeros((), jnp.float32), (token_set, segment_ids))
        return result
    result, pull_back = jax.vjp(whole_layer, weights, inputs)
    weight_grads, token_grads = pull_back(out_grad.astype(jnp.float32))
    grad_n1g, grad_n1b, grad_qkv, grad_qb, grad_vb, grad_wout, grad_ob, grad_n2g, grad_n2b, grad_win, grad_inb, grad_wback, grad_backb = weight_grads
    return (result.astype(jnp.bfloat16), token_grads.astype(jnp.bfloat16), grad_n1g, grad_n1b, grad_qkv, grad_qb, grad_vb, grad_wout, grad_ob, grad_n2g, grad_n2b, grad_win, grad_inb, grad_wback, grad_backb)
```

```python
import jax
import jax.numpy as jnp
from jax import lax
from jax.sharding import PartitionSpec as P

D = 768
HEADS = 12
HEAD_DIM = 64
HEAD_GRP = 4
BF = jnp.bfloat16
F32 = jnp.float32


def xor_send(value, axis, mask):
    size = lax.axis_size(axis)
    return lax.ppermute(value, axis, [(i, i ^ mask) for i in range(size)])


def pick(stacked, index):
    return lax.dynamic_index_in_dim(stacked, index, 0, keepdims=False)


def reduce_shard(grad):
    size = lax.axis_size("shard")
    me = lax.axis_index("shard")
    rows = grad.shape[0] // size
    part = grad.reshape(size, rows, grad.shape[1])
    bit = 1
    while bit < size:
        split = part.reshape(part.shape[0] // 2, 2, rows, grad.shape[1])
        own = (me // bit) % 2
        sent = lax.dynamic_index_in_dim(split, 1 - own, 1, keepdims=False).astype(BF)
        kept = lax.dynamic_index_in_dim(split, own, 1, keepdims=False)
        part = kept + xor_send(sent, "shard", bit).astype(F32)
        bit *= 2
    return part[0]


def scatter_axis(part, axis):
    size = lax.axis_size(axis)
    me = lax.axis_index(axis)
    pieces = part.reshape(size, part.shape[0] // size, part.shape[1])
    total = pick(pieces, me)
    for mask in range(1, size):
        total = total + xor_send(pick(pieces, me ^ mask).astype(BF), axis, mask).astype(F32)
    return total


def gather_axis(piece, axis):
    size = lax.axis_size(axis)
    me = lax.axis_index(axis)
    rows = piece.shape[0]
    whole = jnp.zeros((size * rows, piece.shape[1]), piece.dtype)
    whole = lax.dynamic_update_slice(whole, piece, (me * rows, 0))
    for mask in range(1, size):
        whole = lax.dynamic_update_slice(
            whole, xor_send(piece, axis, mask), ((me ^ mask) * rows, 0)
        )
    return whole


def reduce_grad(grad):
    part = reduce_shard(grad)
    part = scatter_axis(part, "seq")
    part = scatter_axis(part, "rep").astype(BF)
    part = gather_axis(part, "rep")
    return gather_axis(part, "seq").astype(F32)


def sum_all(value):
    for axis in ("shard", "seq", "rep"):
        bit = 1
        while bit < lax.axis_size(axis):
            value = value + xor_send(value, axis, bit)
            bit *= 2
    return value


def norm_stats(inputs):
    row_mean = jnp.mean(inputs, axis=-1, keepdims=True)
    centered = inputs - row_mean
    row_var = jnp.mean(centered * centered, axis=-1, keepdims=True)
    rstd = lax.rsqrt(row_var + 1e-06)
    return centered * rstd, rstd


def norm_back(in_grad, normal, rstd, gain):
    scaled = in_grad * gain
    mean_e = jnp.mean(scaled, axis=-1, keepdims=True)
    mean_en = jnp.mean(scaled * normal, axis=-1, keepdims=True)
    return rstd * (scaled - mean_e - normal * mean_en)


def inner_rows(left, right):
    return lax.dot_general(
        left, right, (((0,), (0,)), ((), ())), preferred_element_type=jnp.float32
    )


def times_trans(left, right):
    return lax.dot_general(
        left, right, (((1,), (1,)), ((), ())), preferred_element_type=jnp.float32
    )


def times(left, right):
    return jnp.dot(left, right, preferred_element_type=jnp.float32)


def head_scores(query_grp, key_grp, allowed):
    scores = jnp.einsum(
        "qhd,khd->hqk", query_grp, key_grp, preferred_element_type=jnp.float32
    ) * HEAD_DIM ** (-0.5)
    return jnp.where(allowed[None], scores, -1e30)


def attention(qkv_rows, ids):
    rows = qkv_rows.shape[0]
    allowed = ids[:, None] == ids[None, :]
    cols = HEAD_GRP * HEAD_DIM
    mixed_parts, lse_parts = [], []
    for group in range(HEADS // HEAD_GRP):
        lo = group * cols
        query_grp, key_grp, value_grp = (
            qkv_rows[:, at + lo : at + lo + cols].reshape(rows, HEAD_GRP, HEAD_DIM)
            for at in (0, D, 2 * D)
        )
        scores = head_scores(query_grp, key_grp, allowed)
        top = jnp.max(scores, axis=-1, keepdims=True)
        expo = jnp.exp(scores - top)
        total = jnp.sum(expo, axis=-1, keepdims=True)
        probs_low = (expo / total).astype(BF)
        mixed = jnp.einsum("hqk,khd->qhd", probs_low, value_grp, preferred_element_type=F32)
        mixed_parts.append(mixed.reshape(rows, cols))
        lse_parts.append(top + jnp.log(total))
    return jnp.concatenate(mixed_parts, axis=1).astype(BF), lse_parts


def attention_back(qkv_rows, ids, attn, lse_parts, attn_grad):
    rows = qkv_rows.shape[0]
    allowed = ids[:, None] == ids[None, :]
    cols = HEAD_GRP * HEAD_DIM
    query_parts, key_parts, value_parts = [], [], []
    for group in range(HEADS // HEAD_GRP):
        lo = group * cols
        query_grp, key_grp, value_grp = (
            qkv_rows[:, at + lo : at + lo + cols].reshape(rows, HEAD_GRP, HEAD_DIM)
            for at in (0, D, 2 * D)
        )
        probs = jnp.exp(head_scores(query_grp, key_grp, allowed) - lse_parts[group])
        probs_low = probs.astype(BF)
        attn_grp = attn_grad[:, lo : lo + cols].reshape(rows, HEAD_GRP, HEAD_DIM)
        value_grad = jnp.einsum("hqk,qhd->khd", probs_low, attn_grp, preferred_element_type=F32)
        prob_grad = jnp.einsum("qhd,khd->hqk", attn_grp, value_grp, preferred_element_type=F32)
        row_inner = jnp.sum(prob_grad * probs, axis=-1, keepdims=True)
        score_grad = (probs * (prob_grad - row_inner)).astype(BF)
        query_grad = jnp.einsum("hqk,khd->qhd", score_grad, key_grp, preferred_element_type=F32)
        key_grad = jnp.einsum("hqk,qhd->khd", score_grad, query_grp, preferred_element_type=F32)
        scale = HEAD_DIM ** (-0.5)
        query_parts.append((query_grad * scale).reshape(rows, cols))
        key_parts.append((key_grad * scale).reshape(rows, cols))
        value_parts.append(value_grad.reshape(rows, cols))
    return jnp.concatenate(query_parts + key_parts + value_parts, axis=1).astype(BF)


def swap_halves(halves, me):
    size = lax.axis_size("seq")
    whole = jnp.zeros_like(halves)
    whole = lax.dynamic_update_slice(whole, pick(halves, me)[None], (me, 0, 0))
    for mask in range(1, size):
        got = xor_send(pick(halves, me ^ mask), "seq", mask)
        whole = lax.dynamic_update_slice(whole, got[None], (me ^ mask, 0, 0))
    return whole


def layer(params, tokens, ids, out_grad):
    (w_qkv, w_out, w_in, w_back, vectors) = params
    n1_gain, n1_bias, q_bias, v_bias, o_bias, n2_gain, n2_bias, back_bias, in_bias = vectors
    resid_in = tokens.astype(F32)
    normal1, rstd1 = norm_stats(resid_in)
    normed1 = (normal1 * n1_gain + n1_bias).astype(BF)
    qkv_shift = jnp.concatenate([q_bias, jnp.zeros_like(q_bias), v_bias])
    qkv_rows = (times(normed1, w_qkv) + qkv_shift).astype(BF)
    attn, lse = attention(qkv_rows, ids)
    resid_mid = resid_in + times(attn, w_out) + o_bias
    normal2, rstd2 = norm_stats(resid_mid)
    normed2 = (normal2 * n2_gain + n2_bias).astype(BF)
    pre_act = times(normed2, w_in) + in_bias
    cdf = 0.5 * (1.0 + lax.erf(pre_act * 0.7071067811865476))
    hidden = (pre_act * cdf).astype(BF)
    block_out = (resid_mid + times(hidden, w_back) + back_bias).astype(BF)

    g_backb = jnp.sum(out_grad, axis=0, dtype=F32)
    g_wback = reduce_grad(inner_rows(hidden, out_grad))
    slope = cdf + pre_act * (0.3989422804014327 * jnp.exp(-0.5 * pre_act * pre_act))
    pre_grad = (times_trans(out_grad, w_back) * slope).astype(BF)
    g_inb = jnp.sum(pre_grad, axis=0, dtype=F32)
    g_win = reduce_grad(inner_rows(normed2, pre_grad))
    n2_grad = times_trans(pre_grad, w_in)
    g_n2g = jnp.sum(n2_grad * normal2, axis=0)
    g_n2b = jnp.sum(n2_grad, axis=0)
    mid_grad = out_grad.astype(F32) + norm_back(n2_grad, normal2, rstd2, n2_gain)
    branch = mid_grad.astype(BF)
    g_ob = jnp.sum(branch, axis=0, dtype=F32)
    g_wout = reduce_grad(inner_rows(attn, branch))
    attn_grad = times_trans(branch, w_out).astype(BF)
    qkv_grad = attention_back(qkv_rows, ids, attn, lse, attn_grad)
    g_qb = jnp.sum(qkv_grad[:, :D], axis=0, dtype=F32)
    g_vb = jnp.sum(qkv_grad[:, 2 * D :], axis=0, dtype=F32)
    g_qkv = reduce_grad(inner_rows(normed1, qkv_grad))
    n1_grad = times_trans(qkv_grad, w_qkv)
    g_n1g = jnp.sum(n1_grad * normal1, axis=0)
    g_n1b = jnp.sum(n1_grad, axis=0)
    token_grad = (mid_grad + norm_back(n1_grad, normal1, rstd1, n1_gain)).astype(BF)
    small = (g_n1g, g_n1b, g_qb, g_vb, g_ob, g_n2g, g_n2b, g_backb, g_inb)
    return block_out, token_grad, (g_qkv, g_wout, g_win, g_wback), small


def body(
    tokens,
    segment_ids,
    out_grad,
    norm1_gain,
    norm1_bias,
    qkv_weight,
    query_bias,
    value_bias,
    out_weight,
    out_bias,
    norm2_gain,
    norm2_bias,
    ff_in_weight,
    ff_in_bias,
    ff_out_weight,
    ff_out_bias,
):
    seqs, row_count, _ = tokens.shape
    ways = lax.axis_size("seq")
    me = lax.axis_index("seq")
    shards = lax.axis_size("shard")
    shard = lax.axis_index("shard")
    cell = norm1_gain.shape[0]

    vec = jnp.concatenate(
        [
            norm1_gain,
            norm1_bias,
            query_bias,
            value_bias,
            out_bias,
            norm2_gain,
            norm2_bias,
            ff_out_bias,
            ff_in_bias,
        ]
    )
    vec_all = lax.all_gather(vec, "shard", axis=0).astype(F32)
    w_qkv = lax.all_gather(qkv_weight, "shard", axis=0, tiled=True)
    w_out = lax.all_gather(out_weight, "shard", axis=0, tiled=True)
    w_in = lax.all_gather(ff_in_weight, "shard", axis=0, tiled=True)
    w_back = lax.all_gather(ff_out_weight, "shard", axis=0, tiled=True)
    vectors = [vec_all[:, i * cell : (i + 1) * cell].reshape(-1) for i in range(8)]
    vectors.append(vec_all[:, 8 * cell :].reshape(-1))
    params = (w_qkv, w_out, w_in, w_back, vectors)

    out_parts, grad_parts = [], []
    weight_totals, small_totals = None, None
    for group in range(seqs // ways):
        lo = group * ways
        rows = swap_halves(tokens[lo : lo + ways], me).reshape(ways * row_count, -1)
        cots = swap_halves(out_grad[lo : lo + ways], me).reshape(ways * row_count, -1)
        ids = pick(segment_ids[lo : lo + ways], me)
        block, tgrad, grads, small = layer(params, rows, ids, cots)
        out_parts.append(swap_halves(block.reshape(ways, row_count, -1), me))
        grad_parts.append(swap_halves(tgrad.reshape(ways, row_count, -1), me))
        if group == 0:
            weight_totals, small_totals = grads, small
        else:
            weight_totals = jax.tree.map(jnp.add, weight_totals, grads)
            small_totals = jax.tree.map(jnp.add, small_totals, small)
    g_qkv, g_wout, g_win, g_wback = weight_totals
    packed = jnp.concatenate([s.reshape(shards, -1) for s in small_totals], axis=1)
    mine = pick(sum_all(packed), shard)
    s = [mine[i * cell : (i + 1) * cell] for i in range(8)] + [mine[8 * cell :]]
    return (
        jnp.concatenate(out_parts, axis=0),
        jnp.concatenate(grad_parts, axis=0),
        s[0],
        s[1],
        g_qkv,
        s[2],
        s[3],
        g_wout,
        s[4],
        s[5],
        s[6],
        g_win,
        s[8],
        g_wback,
        s[7],
    )


def solution(mesh):
    in_specs = (
        P(("shard", "rep"), "seq", None),
        P(("shard", "rep"), None),
        P(("shard", "rep"), "seq", None),
        P("shard"),
        P("shard"),
        P("shard", None),
        P("shard"),
        P("shard"),
        P("shard", None),
        P("shard"),
        P("shard"),
        P("shard"),
        P("shard", None),
        P("shard"),
        P("shard", None),
        P("shard"),
    )
    out_specs = (
        P(("shard", "rep"), "seq", None),
        P(("shard", "rep"), "seq", None),
        P("shard"),
        P("shard"),
        P("shard", None),
        P("shard"),
        P("shard"),
        P("shard", None),
        P("shard"),
        P("shard"),
        P("shard"),
        P("shard", None),
        P("shard"),
        P("shard", None),
        P("shard"),
    )
    return jax.shard_map(body, mesh=mesh, in_specs=in_specs, out_specs=out_specs, check_vma=False)
```

```python
import jax
import jax.numpy as jnp
from jax import lax
from jax.experimental import pallas as pl
from jax.experimental.pallas import tpu as pltpu
from jax.sharding import PartitionSpec as P

D = 768
HEADS = 12
HEAD_DIM = 64
LANES = 128
HB = 512
PAIRS = HEADS // 2
FAR = -1e30
BF = jnp.bfloat16
F32 = jnp.float32
MIB = 1 << 20


def xor_send(value, axis, mask):
    size = lax.axis_size(axis)
    return lax.ppermute(value, axis, [(i, i ^ mask) for i in range(size)])


def bits(axis):
    return [(axis, 1 << b) for b in range((lax.axis_size(axis) - 1).bit_length())]


def bit_of(axis, mask):
    return (lax.axis_index(axis) // mask) % 2


def pick(stacked, index):
    return lax.dynamic_index_in_dim(stacked, index, 0, keepdims=False)


def tie(*values):
    return lax.optimization_barrier(values)


def added(state):
    return (state[0].astype(F32) + state[1].astype(F32)).astype(BF)


def halve(state, step, dim):
    axis, mask = step
    bit = bit_of(axis, mask)
    size = state[0].shape[dim] // 2
    cut = lambda at: added([lax.dynamic_slice_in_dim(s, at * size, size, dim) for s in state])
    return cut(bit), xor_send(cut(1 - bit), axis, mask)


def whole(state, step):
    value = added(state)
    return value, xor_send(value, *step)


def join(part, step, dim):
    bit = bit_of(*step)
    other = xor_send(part, *step)
    low = jnp.where(bit == 0, part, other)
    high = jnp.where(bit == 0, other, part)
    return jnp.concatenate([low, high], axis=dim)


def chips(state):
    mask = 2
    while mask < lax.axis_size("shard"):
        state = halve_blocks(state, mask)
        mask *= 2
    return state


def halve_blocks(state, mask):
    bit = bit_of("shard", mask)

    def cut(at):
        split = [s.reshape((s.shape[0] // 2, 2) + s.shape[1:]) for s in state]
        return added([lax.dynamic_index_in_dim(s, at, 1, keepdims=False) for s in split])

    return cut(bit), xor_send(cut(1 - bit), "shard", mask)


def swap_halves(halves, me):
    size = lax.axis_size("seq")
    if size == 2:
        kept, got = pick(halves, me), xor_send(pick(halves, 1 - me), "seq", 1)
        return jnp.stack([jnp.where(me == 0, kept, got), jnp.where(me == 0, got, kept)])
    out = jnp.zeros_like(halves)
    out = lax.dynamic_update_slice(out, pick(halves, me)[None], (me, 0, 0))
    for mask in range(1, size):
        got = xor_send(pick(halves, me ^ mask), "seq", mask)
        out = lax.dynamic_update_slice(out, got[None], (me ^ mask, 0, 0))
    return out


def quarters(full):
    rows = full.shape[0] // 4
    return [full[k * rows : (k + 1) * rows] for k in range(4)]


def part_axes(shard):
    parts = bits("rep")[:1] + bits("seq")
    return parts if shard.shape[0] % (8 << len(parts)) == 0 else []


def fetch_part(shard, parts):
    piece = shard
    for axis, mask in parts:
        half = piece.shape[0] // 2
        piece = lax.dynamic_slice_in_dim(piece, bit_of(axis, mask) * half, half)
    return xor_send(piece, "shard", 2)


def cost(flops, bytes_accessed, transcendentals):
    return pl.CostEstimate(
        flops=flops, bytes_accessed=bytes_accessed, transcendentals=transcendentals
    )


def sds(shape, dtype):
    return jax.ShapeDtypeStruct(shape, dtype)


def fixed(shape):
    return pl.BlockSpec(shape, lambda i: (0,) * len(shape), pipeline_mode=pl.Buffered(1))


def contract(left, right, dims):
    return lax.dot_general(left, right, (dims, ((), ())), preferred_element_type=F32)


def row_stats(rows):
    mean = jnp.mean(rows, axis=-1, keepdims=True)
    centered = rows - mean
    rstd = lax.rsqrt(jnp.mean(centered * centered, axis=-1, keepdims=True) + 1e-06)
    return centered * rstd, rstd


def norm_back(in_grad, normal, rstd, gain):
    scaled = in_grad * gain
    mean_e = jnp.mean(scaled, axis=-1, keepdims=True)
    mean_en = jnp.mean(scaled * normal, axis=-1, keepdims=True)
    return rstd * (scaled - mean_e - normal * mean_en)


def put_parities(value, parity, keep_ref, send_ref, at):
    blocks, rows = keep_ref.shape[0], keep_ref.shape[1]
    cols = pl.ds(at, value.shape[1])
    for k in range(blocks):
        even = value[2 * k * rows : (2 * k + 1) * rows]
        odd = value[(2 * k + 1) * rows : (2 * k + 2) * rows]
        keep_ref[k, :, cols] = jnp.where(parity == 0, even, odd).astype(BF)
        send_ref[k, :, cols] = jnp.where(parity == 0, odd, even).astype(BF)


def place(ref, blocks, position):
    rows = blocks[0].shape[0]
    for k, block in enumerate(blocks):
        at = pl.multiple_of((position ^ k) * rows, rows)
        ref[pl.ds(at, rows), :] = block[...]


def first_kernel(pos_ref, tok_ref, gain_ref, shift_ref, w0, w1, w2, w3, bias_ref, qkv_ref, turned_ref, w_ref, normed_ref):
    @pl.when(pl.program_id(0) == 0)
    def _():
        n, _ = row_stats(tok_ref[...].astype(F32))
        x = (n * gain_ref[...] + shift_ref[...]).astype(BF)
        normed_ref[...] = x
        turned_ref[...] = x.T

    place(w_ref, (w0, w1, w2, w3), pos_ref[0])
    qkv_ref[...] = (contract(normed_ref[...], w_ref[...], ((1,), (0,))) + bias_ref[...]).astype(BF)


def first(position, tokens, gain, shift, blocks, bias):
    rows = tokens.shape[0]
    block = pl.BlockSpec((D // 4, D), lambda i: (0, i))
    return pl.pallas_call(
        first_kernel,
        grid=(3,),
        in_specs=[
            pl.BlockSpec(memory_space=pltpu.SMEM),
            fixed((rows, D)),
            fixed((1, D)),
            fixed((1, D)),
            block,
            block,
            block,
            block,
            pl.BlockSpec((1, D), lambda i: (0, i)),
        ],
        out_specs=[
            pl.BlockSpec((rows, D), lambda i: (0, i)),
            fixed((D, rows)),
            pl.BlockSpec((D, D), lambda i: (0, i)),
        ],
        out_shape=[sds((rows, 3 * D), BF), sds((D, rows), BF), sds((D, 3 * D), BF)],
        scratch_shapes=[pltpu.VMEM((rows, D), BF)],
        cost_estimate=cost(6 * rows * D * D, 10 * rows * D + 12 * D * D, rows),
        compiler_params=pltpu.CompilerParams(vmem_limit_bytes=62 * MIB),
        name="norm_and_projections",
    )(position, tokens, gain, shift, *blocks, bias)


def by_head(rows):
    lane = lax.broadcasted_iota(jnp.int32, rows.shape, 1)
    zero = jnp.zeros_like(rows)
    return jnp.concatenate(
        [jnp.where(lane < HEAD_DIM, rows, zero), jnp.where(lane >= HEAD_DIM, rows, zero)], axis=0
    )


def own_rows(both, width):
    return jnp.concatenate([both[:HEAD_DIM, :width], both[HEAD_DIM:, width:]], axis=0)


def query_side(q_ref, hot_ref):
    hot = hot_ref[...]
    q = by_head(q_ref[...] * jnp.asarray(HEAD_DIM**-0.5, BF))
    return jnp.concatenate([q, jnp.concatenate([hot, hot], axis=0)], axis=1)


def attn_fwd_kernel(q_ref, k_ref, v_ref, hot_ref, far_ref, *rest):
    o_ref, lse_ref = rest[-2:]
    width = q_ref.shape[0]
    qs = query_side(q_ref, hot_ref)
    ks = jnp.concatenate([k_ref[...], far_ref[...]], axis=1)
    s = contract(ks, qs, ((1,), (1,)))
    top = jnp.max(s, axis=0, keepdims=True)
    e = jnp.exp(s - top)
    tot = jnp.sum(e, axis=0, keepdims=True)
    p = (e * (1.0 / tot)).astype(BF)
    o = contract(v_ref[...], p, ((0,), (0,)))
    o_ref[...] = own_rows(o, width).T.astype(BF)
    lse_ref[0] = top + jnp.log(tot)


def pair_cols(rows, at):
    return pl.BlockSpec((rows, LANES), lambda p: (0, at + p))


def attn_fwd(qkv, hot, far, at, count, before=()):
    rows = qkv.shape[0]
    return pl.pallas_call(
        attn_fwd_kernel,
        grid=(count,),
        in_specs=[
            pair_cols(rows, at),
            pair_cols(rows, PAIRS + at),
            pair_cols(rows, 2 * PAIRS + at),
            fixed((rows, LANES)),
            fixed((rows, LANES)),
        ]
        + [pl.BlockSpec(memory_space=pl.ANY)] * len(before),
        out_specs=[pair_cols(rows, at), pl.BlockSpec((1, 1, 2 * rows), lambda p: (at + p, 0, 0))],
        out_shape=[sds((rows, D), BF), sds((PAIRS, 1, 2 * rows), F32)],
        input_output_aliases={5 + i: i for i in range(len(before))},
        cost_estimate=cost(
            16 * rows * rows * LANES * count, 8 * rows * LANES * count, 2 * count * rows * rows
        ),
        compiler_params=pltpu.CompilerParams(vmem_limit_bytes=62 * MIB),
        name="attention_forward",
    )(qkv, qkv, qkv, hot, far, *before)


def attn_bwd_kernel(
    q_ref, k_ref, v_ref, do_ref, hot_ref, far_ref, lse_ref, *rest
):
    grad_ref = rest[-1]
    width = q_ref.shape[0]
    qs = query_side(q_ref, hot_ref)
    do = by_head(do_ref[...])
    keys = k_ref[...]
    ks = jnp.concatenate([keys, far_ref[...]], axis=1)
    s = contract(ks, qs, ((1,), (1,)))
    p = jnp.exp(s - lse_ref[0])
    dp = contract(v_ref[...], do, ((1,), (1,)))
    t = p * dp
    inner = jnp.sum(t, axis=0, keepdims=True)
    ds = (t - p * inner).astype(BF)
    grad_ref[2] = contract(p.astype(BF), do, ((1,), (0,))).astype(BF)
    grad_ref[1] = contract(ds, qs[:, :LANES], ((1,), (0,))).astype(BF)
    dq = own_rows(contract(keys, ds, ((0,), (0,))), width)
    grad_ref[0] = (dq * HEAD_DIM**-0.5).T.astype(BF)


def attn_bwd(qkv, dout, hot, far, lse, at, count, before=()):
    rows = qkv.shape[0]
    return pl.pallas_call(
        attn_bwd_kernel,
        grid=(count,),
        in_specs=[
            pair_cols(rows, at),
            pair_cols(rows, PAIRS + at),
            pair_cols(rows, 2 * PAIRS + at),
            pair_cols(rows, at),
            fixed((rows, LANES)),
            fixed((rows, LANES)),
            pl.BlockSpec((1, 1, 2 * rows), lambda p: (at + p, 0, 0)),
        ]
        + [pl.BlockSpec(memory_space=pl.ANY)] * len(before),
        out_specs=pl.BlockSpec((3, rows, LANES), lambda p: (0, 0, at + p)),
        out_shape=sds((3, rows, D), BF),
        input_output_aliases={7 + i: i for i in range(len(before))},
        cost_estimate=cost(
            10 * rows * rows * LANES * count * 4, 14 * rows * LANES * count, 2 * count * rows * rows
        ),
        compiler_params=pltpu.CompilerParams(vmem_limit_bytes=62 * MIB),
        name="attention_backward",
    )(qkv, qkv, qkv, dout, hot, far, lse, *before)


def middle_kernel(
    par_ref, tok_ref, attn_ref, g_ref, wo_ref, ob_ref, gain_ref, shift_ref, bb_ref, wi_ref, ib_ref, wb_ref,
    out_ref, mid_ref, agrad_ref, keep_ref, send_ref, gwb_ref, gib_ref, small_ref,
    resid, normed, normed_t, out_acc, in_acc,
):
    i = pl.program_id(0)
    parity = par_ref[1]

    @pl.when(i == 0)
    def _():
        r = tok_ref[...].astype(F32) + contract(attn_ref[...], wo_ref[...], ((1,), (0,))) + ob_ref[...]
        resid[...] = r
        n, _ = row_stats(r)
        x = (n * gain_ref[...] + shift_ref[...]).astype(BF)
        normed[...] = x
        normed_t[...] = x.T
        out_acc[...] = jnp.zeros_like(out_acc)
        in_acc[...] = jnp.zeros_like(in_acc)

    x = normed[...]
    g = g_ref[...]
    wi = wi_ref[...]
    wb = wb_ref[...]
    pre = contract(x, wi, ((1,), (0,))) + ib_ref[...]
    cdf = 0.5 + 0.5 * lax.erf(pre * 0.7071067811865476)
    h = (pre * cdf).astype(BF)
    slope = cdf + pre * (0.3989422804014327 * jnp.exp(-0.5 * (pre * pre)))
    pg = (contract(g, wb, ((1,), (1,))) * slope).astype(BF)
    out_acc[...] += contract(h, wb, ((1,), (0,)))
    in_acc[...] += contract(pg, wi, ((1,), (1,)))
    at = pl.multiple_of(i * HB, HB)
    put_parities(contract(normed_t[...], pg, ((1,), (0,))), parity, keep_ref, send_ref, at)
    gwb_ref[...] = contract(h, g, ((0,), (0,))).astype(BF)
    gib_ref[...] = jnp.sum(pg.astype(F32), axis=0, keepdims=True)

    @pl.when(i == pl.num_programs(0) - 1)
    def _():
        r = resid[...]
        out_ref[...] = (r + out_acc[...] + bb_ref[...]).astype(BF)
        n, rstd = row_stats(r)
        d = in_acc[...]
        gf = g_ref[...].astype(F32)
        m = gf + norm_back(d, n, rstd, gain_ref[...])
        mid_ref[...] = m
        b = m.astype(BF)
        small_ref[0:1, :] = jnp.sum(b.astype(F32), axis=0, keepdims=True)
        small_ref[1:2, :] = jnp.sum(d * n, axis=0, keepdims=True)
        small_ref[2:3, :] = jnp.sum(d, axis=0, keepdims=True)
        small_ref[3:4, :] = jnp.sum(gf, axis=0, keepdims=True)
        agrad_ref[...] = contract(b, wo_ref[...], ((1,), (1,))).astype(BF)
        put_parities(
            contract(attn_ref[...], b, ((0,), (0,))), parity, keep_ref, send_ref,
            keep_ref.shape[2] - D,
        )


def middle(parity, tokens, attn, grad, w_out, o_bias, gain, shift, back_bias, w_in, in_bias, w_back):
    rows = tokens.shape[0]
    ff = w_in.shape[1]
    shards = lax.axis_size("shard")
    half = (shards // 2, D // shards, ff + D)
    return pl.pallas_call(
        middle_kernel,
        grid=(ff // HB,),
        in_specs=[
            pl.BlockSpec(memory_space=pltpu.SMEM),
            fixed((rows, D)),
            fixed((rows, D)),
            fixed((rows, D)),
            fixed((D, D)),
            fixed((1, D)),
            fixed((1, D)),
            fixed((1, D)),
            fixed((1, D)),
            pl.BlockSpec((D, HB), lambda i: (0, i)),
            pl.BlockSpec((1, HB), lambda i: (0, i)),
            pl.BlockSpec((HB, D), lambda i: (i, 0)),
        ],
        out_specs=[
            fixed((rows, D)),
            fixed((rows, D)),
            fixed((rows, D)),
            fixed(half),
            fixed(half),
            pl.BlockSpec((HB, D), lambda i: (i, 0)),
            pl.BlockSpec((1, HB), lambda i: (0, i)),
            fixed((8, D)),
        ],
        out_shape=[
            sds((rows, D), BF),
            sds((rows, D), F32),
            sds((rows, D), BF),
            sds(half, BF),
            sds(half, BF),
            sds((ff, D), BF),
            sds((1, ff), F32),
            sds((8, D), F32),
        ],
        scratch_shapes=[
            pltpu.VMEM((rows, D), F32),
            pltpu.VMEM((rows, D), BF),
            pltpu.VMEM((D, rows), BF),
            pltpu.VMEM((rows, D), F32),
            pltpu.VMEM((rows, D), F32),
        ],
        cost_estimate=cost(2 * rows * D * (6 * ff + 3 * D), 10 * D * ff + 20 * rows * D, 2 * rows * ff),
        compiler_params=pltpu.CompilerParams(vmem_limit_bytes=62 * MIB),
        name="projection_and_feed_forward",
    )(parity, tokens, attn, grad, w_out, o_bias, gain, shift, back_bias, w_in, in_bias, w_back)


def last_kernel(
    par_ref, tok_ref, turned_ref, mid_ref, d_ref, w_ref, gain_ref, small_ref, gib_ref,
    tgrad_ref, keep_ref, send_ref, wkeep_ref, wsend_ref, total, columns,
):
    i = pl.program_id(0)
    parity = par_ref[1]
    d = d_ref[0]

    @pl.when(i == 0)
    def _():
        columns[...] = jnp.zeros_like(columns)
        columns[4:8, :] = small_ref[0:4, :]
        columns[8 : 8 + gib_ref.shape[0], :] = gib_ref[...]
        total[...] = jnp.zeros_like(total)
        columns[2:3, :] = jnp.sum(d.astype(F32), axis=0, keepdims=True)

    put_parities(contract(turned_ref[...], d, ((1,), (0,))), parity, keep_ref, send_ref, 0)
    total[...] += contract(d, w_ref[...], ((1,), (1,)))

    @pl.when(i == 2)
    def _():
        columns[3:4, :] = jnp.sum(d.astype(F32), axis=0, keepdims=True)
        t = total[...]
        n, rstd = row_stats(tok_ref[...].astype(F32))
        tgrad_ref[...] = (mid_ref[...] + norm_back(t, n, rstd, gain_ref[...])).astype(BF)
        columns[0:1, :] = jnp.sum(t * n, axis=0, keepdims=True)
        columns[1:2, :] = jnp.sum(t, axis=0, keepdims=True)
        put_parities(columns[...].T, parity, wkeep_ref, wsend_ref, 0)


def last(scalars, tokens, turned, mid_grad, grads, w_qkv, gain, small, g_inb):
    rows = tokens.shape[0]
    shards = lax.axis_size("shard")
    half = (shards // 2, D // shards, 3 * D)
    thin = (shards // 2, D // shards, LANES)
    part = pl.BlockSpec((shards // 2, D // shards, D), lambda i: (0, 0, i))
    return pl.pallas_call(
        last_kernel,
        grid=(3,),
        in_specs=[
            pl.BlockSpec(memory_space=pltpu.SMEM),
            fixed((rows, D)),
            fixed((D, rows)),
            fixed((rows, D)),
            pl.BlockSpec((1, rows, D), lambda i: (i, 0, 0)),
            pl.BlockSpec((D, D), lambda i: (0, i)),
            fixed((1, D)),
            fixed((8, D)),
            fixed(g_inb.shape),
        ],
        out_specs=[fixed((rows, D)), part, part, fixed(thin), fixed(thin)],
        out_shape=[sds((rows, D), BF), sds(half, BF), sds(half, BF), sds(thin, BF), sds(thin, BF)],
        scratch_shapes=[pltpu.VMEM((rows, D), F32), pltpu.VMEM((LANES, D), F32)],
        cost_estimate=cost(12 * rows * D * D, 18 * rows * D + 12 * D * D, rows),
        compiler_params=pltpu.CompilerParams(vmem_limit_bytes=62 * MIB),
        name="projections_backward",
    )(scalars, tokens, turned, mid_grad, grads, w_qkv, gain, small, g_inb)


def by_shard(vector):
    shards = lax.axis_size("shard")
    count = vector.shape[1] // D
    return vector.reshape(shards, count, D // shards).transpose(1, 0, 2).reshape(count, D)


def row(vector):
    return vector.reshape(1, -1)


def in_order(blocks, position):
    rows = blocks[0].shape[0]
    out = jnp.zeros((len(blocks) * rows, blocks[0].shape[1]), blocks[0].dtype)
    for k, block in enumerate(blocks):
        out = lax.dynamic_update_slice(out, block, ((position ^ k) * rows, 0))
    return out


def layer(shards, params, halves, ids, out_halves):
    params, qkv_shard, out_shard, in_shard, back_shard = (params, *shards)
    rows = halves.shape[0] * halves.shape[1]
    me = lax.axis_index("seq")
    count = lax.axis_size("shard")
    mine = lax.axis_index("shard").astype(jnp.int32)
    near, far_axis = bits("seq")[0], bits("rep")
    direct = count == 4
    position = mine if direct else jnp.int32(0)
    scalars = jnp.stack([position, mine % 2])
    gather = lambda w: lax.all_gather(w, "shard", axis=0, tiled=True)
    to_core = lambda w: xor_send(w, "shard", 1)

    tokens = swap_halves(halves, me).reshape(rows, D)
    if direct:
        split = part_axes(back_shard)
        across = xor_send(qkv_shard, "shard", 2)
        beside = to_core(qkv_shard)
        across, tokens, out_shard, in_shard, back_shard, *params = tie(
            across, tokens, out_shard, in_shard, back_shard, *params
        )
        w_qkv = [qkv_shard, beside, across, to_core(across)]
        back_piece = fetch_part(back_shard, split)
        out_across = xor_send(out_shard, "shard", 2)
        out_beside, back_beside = to_core(out_shard), to_core(back_shard)
    else:
        w_qkv = quarters(gather(qkv_shard))
    n1_gain, n1_bias, q_bias, v_bias, o_bias, n2_gain, n2_bias, back_bias, in_bias = params
    w_in = gather(in_shard)
    bias = jnp.concatenate([q_bias, jnp.zeros_like(q_bias), v_bias])
    qkv, turned, w_qkv = first(scalars, tokens, row(n1_gain), row(n1_bias), w_qkv, row(bias))
    same = ids[:, None] == jnp.arange(LANES, dtype=ids.dtype)[None, :]
    hot = same.astype(BF)
    far = jnp.where(same, 0.0, FAR).astype(BF)
    qkv, out_halves = tie(qkv, out_halves)
    got_grad = xor_send(pick(out_halves, 1 - me), "seq", 1)
    if direct:
        qkv, back_piece, out_across, out_beside, back_beside = tie(
            qkv, back_piece, out_across, out_beside, back_beside
        )
        w_out = [out_shard, out_beside, out_across, to_core(out_across)]
    for step in reversed(split[1:] if direct else []):
        back_piece = join(back_piece, step, 0)
    attn = attn_fwd(qkv, hot, far, 0, PAIRS // 2)
    if direct:
        *attn, back_piece, w_out[3] = tie(*attn, back_piece, w_out[3])
        back_piece = join(back_piece, split[0], 0)
    attn, lse = attn_fwd(qkv, hot, far, PAIRS // 2, PAIRS - PAIRS // 2, attn)
    attn, got_grad, w_in = tie(attn, got_grad, w_in)
    kept_grad = pick(out_halves, me)
    out_grad = jnp.concatenate(
        [jnp.where(me == 0, kept_grad, got_grad), jnp.where(me == 0, got_grad, kept_grad)], axis=0
    )
    if direct:
        attn, back_piece = tie(attn, back_piece)
        w_out = in_order(w_out, position)
        w_back = in_order([back_shard, back_beside, back_piece, to_core(back_piece)], position)
    else:
        w_out = gather(out_shard)
        w_back = gather(back_shard)
    block_out, mid_grad, attn_grad, keep, send, g_wback, g_inb, small = middle(
        scalars, tokens, attn, out_grad, w_out, row(o_bias), row(n2_gain), row(n2_bias),
        row(back_bias), w_in, row(in_bias), w_back,
    )
    back_sum = lax.psum_scatter(g_wback, "shard", scatter_dimension=0, tiled=True)[None]
    got = to_core(send)
    block_out = block_out.reshape(halves.shape)
    got_out = xor_send(pick(block_out, 1 - me), "seq", 1)
    group = PAIRS // 3
    grads = attn_bwd(qkv, attn_grad, hot, far, lse, 0, group)
    grads, got, got_out = tie(grads, got, got_out)
    f = halve((keep, got), near, 1)
    grads = attn_bwd(qkv, attn_grad, hot, far, lse, group, PAIRS - group, [grads])
    grads, back_sum, *f = tie(grads, back_sum, *f)
    f = halve(f, far_axis[0], 1)
    s = halve((back_sum, jnp.zeros_like(back_sum)), near, 1)
    token_grad, keep, send, thin_keep, thin_send = last(
        scalars, tokens, turned, mid_grad, grads, w_qkv, row(n1_gain), small, by_shard(g_inb)
    )
    token_grad, send, thin_send, f, s = tie(token_grad, send, thin_send, f, s)

    t = (keep, to_core(send))
    thin = (thin_keep, to_core(thin_send))
    f = chips(f)
    s = halve(s, far_axis[0], 1)
    t, thin, f, s, token_grad = tie(t, thin, f, s, token_grad)
    cut = 2 * LANES * (3 * D // (4 * LANES))
    a = [v[:, :, :cut] for v in t]
    b = [jnp.concatenate([v[:, :, cut:], w], axis=2) for v, w in zip(t, thin)]
    a, b = chips(a), halve(b, near, 1)
    f, s = last_steps(f, far_axis), last_steps(s, far_axis)
    a, b, token_grad = tie(a, b, token_grad)
    token_grad = token_grad.reshape(halves.shape)
    a, b = halve(a, near, 1), chips(b)
    t = halve([jnp.concatenate([v, w], axis=2) for v, w in zip(a, b)], far_axis[0], 1)
    t, token_grad = tie(t, token_grad)
    got_tokens = xor_send(pick(token_grad, 1 - me), "seq", 1)
    t = last_steps(t, far_axis)
    f, s, t = [join(join(v, far_axis[0], 1), near, 1) for v in (f, s, t)]
    outputs = [
        jnp.stack([jnp.where(me == 0, kept, got), jnp.where(me == 0, got, kept)])
        for kept, got in ((pick(block_out, me), got_out), (pick(token_grad, me), got_tokens))
    ]
    return outputs[0], outputs[1], [v[0].astype(F32) for v in (s, f, t)]


def last_steps(state, order):
    for step in order[1:]:
        state = whole(state, step)
    return added(state)


def body(
    tokens,
    segment_ids,
    out_grad,
    norm1_gain,
    norm1_bias,
    qkv_weight,
    query_bias,
    value_bias,
    out_weight,
    out_bias,
    norm2_gain,
    norm2_bias,
    ff_in_weight,
    ff_in_bias,
    ff_out_weight,
    ff_out_bias,
):
    seqs, row_count, _ = tokens.shape
    ways = lax.axis_size("seq")
    me = lax.axis_index("seq")
    cell = norm1_gain.shape[0]
    wide = ff_in_weight.shape[1]

    vec = jnp.concatenate(
        [
            norm1_gain,
            norm1_bias,
            query_bias,
            value_bias,
            out_bias,
            norm2_gain,
            norm2_bias,
            ff_out_bias,
            ff_in_bias,
        ]
    )
    vec_all = lax.all_gather(vec, "shard", axis=0).astype(F32)
    vectors = [vec_all[:, i * cell : (i + 1) * cell].reshape(-1) for i in range(8)]
    vectors.append(vec_all[:, 8 * cell :].reshape(-1))
    weights = (qkv_weight, out_weight, ff_in_weight, ff_out_weight)

    out_parts, grad_parts, sums = [], [], None
    for lo in range(0, seqs, ways):
        ids = pick(segment_ids[lo : lo + ways], me)
        block, tgrad, terms = layer(
            weights, vectors, tokens[lo : lo + ways], ids, out_grad[lo : lo + ways]
        )
        out_parts.append(block)
        grad_parts.append(tgrad)
        sums = terms if sums is None else [a + b for a, b in zip(sums, terms)]
    g_wback, g_in, g_t = sums
    small = g_t[:, 3 * D : 3 * D + 8 + g_in.shape[1] // D - 1].T
    return (
        jnp.concatenate(out_parts, axis=0),
        jnp.concatenate(grad_parts, axis=0),
        small[0],
        small[1],
        g_t[:, : 3 * D],
        small[2],
        small[3],
        g_in[:, wide:],
        small[4],
        small[5],
        small[6],
        g_in[:, :wide],
        small[8:].reshape(-1),
        g_wback,
        small[7],
    )


def solution(mesh):
    in_specs = (
        P(("shard", "rep"), "seq", None),
        P(("shard", "rep"), None),
        P(("shard", "rep"), "seq", None),
        P("shard"),
        P("shard"),
        P("shard", None),
        P("shard"),
        P("shard"),
        P("shard", None),
        P("shard"),
        P("shard"),
        P("shard"),
        P("shard", None),
        P("shard"),
        P("shard", None),
        P("shard"),
    )
    out_specs = (
        P(("shard", "rep"), "seq", None),
        P(("shard", "rep"), "seq", None),
        P("shard"),
        P("shard"),
        P("shard", None),
        P("shard"),
        P("shard"),
        P("shard", None),
        P("shard"),
        P("shard"),
        P("shard"),
        P("shard", None),
        P("shard"),
        P("shard", None),
        P("shard"),
    )
    return jax.shard_map(body, mesh=mesh, in_specs=in_specs, out_specs=out_specs, check_vma=False)
```

```python
import jax
import jax.numpy as jnp
from jax import lax
from jax.experimental import pallas as pl
from jax.experimental.pallas import tpu as pltpu
from jax.sharding import PartitionSpec as P

D = 768
HEADS = 12
HEAD_DIM = 64
LANES = 128
HB = 512
SPLIT = 2
PAIRS = HEADS // 2
FAR = -1e30
BF = jnp.bfloat16
F32 = jnp.float32
MIB = 1 << 20


def xor_send(value, axis, mask):
    size = lax.axis_size(axis)
    return lax.ppermute(value, axis, [(i, i ^ mask) for i in range(size)])


def bits(axis):
    return [(axis, 1 << b) for b in range((lax.axis_size(axis) - 1).bit_length())]


def bit_of(axis, mask):
    return (lax.axis_index(axis) // mask) % 2


def pick(stacked, index):
    return lax.dynamic_index_in_dim(stacked, index, 0, keepdims=False)


def tie(*values):
    return lax.optimization_barrier(values)


def added(state):
    return (state[0].astype(F32) + state[1].astype(F32)).astype(state[0].dtype)


def cut_half(state, step, dim):
    bit = bit_of(*step)
    size = state[0].shape[dim] // 2
    cut = lambda at: added([lax.dynamic_slice_in_dim(s, at * size, size, dim) for s in state])
    return cut(bit), cut(1 - bit)


def send_half(parts, step):
    return parts[0], xor_send(parts[1], *step)


def halve(state, step, dim):
    return send_half(cut_half(state, step, dim), step)


def whole(state, step):
    value = added(state)
    return value, xor_send(value, *step)


def join(part, step, dim):
    bit = bit_of(*step)
    other = xor_send(part, *step)
    low = jnp.where(bit == 0, part, other)
    high = jnp.where(bit == 0, other, part)
    return jnp.concatenate([low, high], axis=dim)


def cut_chips(state, mask):
    bit = bit_of("shard", mask)

    def cut(at):
        split = [s.reshape((s.shape[0] // 2, 2) + s.shape[1:]) for s in state]
        return added([lax.dynamic_index_in_dim(s, at, 1, keepdims=False) for s in split])

    return cut(bit), cut(1 - bit)


def chips(state, mask=2):
    while mask < lax.axis_size("shard"):
        state = send_half(cut_chips(state, mask), ("shard", mask))
        mask *= 2
    return state


def quarters(full):
    rows = full.shape[0] // 4
    return [full[k * rows : (k + 1) * rows] for k in range(4)]


def part_axes(shard):
    parts = bits("rep")[:1] + bits("seq")
    return parts if shard.shape[0] % (8 << len(parts)) == 0 else []


def fetch_part(shard, parts):
    piece = shard
    for axis, mask in parts:
        half = piece.shape[0] // 2
        piece = lax.dynamic_slice_in_dim(piece, bit_of(axis, mask) * half, half)
    return xor_send(piece, "shard", 2)


def cost(flops, bytes_accessed, transcendentals):
    return pl.CostEstimate(
        flops=flops, bytes_accessed=bytes_accessed, transcendentals=transcendentals
    )


def sds(shape, dtype):
    return jax.ShapeDtypeStruct(shape, dtype)


def fixed(shape):
    return pl.BlockSpec(shape, lambda i: (0,) * len(shape), pipeline_mode=pl.Buffered(1))


def contract(left, right, dims):
    return lax.dot_general(left, right, (dims, ((), ())), preferred_element_type=F32)


def row_stats(rows):
    mean = jnp.mean(rows, axis=-1, keepdims=True)
    centered = rows - mean
    rstd = lax.rsqrt(jnp.mean(centered * centered, axis=-1, keepdims=True) + 1e-06)
    return centered * rstd, rstd


def norm_back(in_grad, normal, rstd, gain):
    scaled = in_grad * gain
    mean_e = jnp.mean(scaled, axis=-1, keepdims=True)
    mean_en = jnp.mean(scaled * normal, axis=-1, keepdims=True)
    return rstd * (scaled - mean_e - normal * mean_en)


def put_parities(value, parity, keep_ref, send_ref, at):
    blocks, rows = keep_ref.shape[0], keep_ref.shape[1]
    cols = pl.ds(at, value.shape[1])
    for k in range(blocks):
        even = value[2 * k * rows : (2 * k + 1) * rows]
        odd = value[(2 * k + 1) * rows : (2 * k + 2) * rows]
        keep_ref[k, :, cols] = jnp.where(parity == 0, even, odd).astype(keep_ref.dtype)
        send_ref[k, :, cols] = jnp.where(parity == 0, odd, even).astype(send_ref.dtype)


def place(ref, blocks, position):
    rows = blocks[0].shape[0]
    for k, block in enumerate(blocks):
        at = pl.multiple_of((position ^ k) * rows, rows)
        ref[pl.ds(at, rows), :] = block[...]


def first_kernel(pos_ref, kept_ref, got_ref, vec_ref, w0, w1, w2, w3, qkv_ref, turned_ref, tok_ref, normed_ref, w_ref):
    i = pl.program_id(0)

    @pl.when(i == 0)
    def _():
        place(tok_ref, (kept_ref.at[0], got_ref), pos_ref[2])
        n, _ = row_stats(tok_ref[...].astype(F32))
        x = (n * vec_ref[0:1, :] + vec_ref[1:2, :]).astype(BF)
        normed_ref[...] = x
        turned_ref[...] = x.T

    place(w_ref, (w0, w1, w2, w3), pos_ref[0])
    bias = jnp.where(i == 0, vec_ref[2:3, :], jnp.where(i == 2, vec_ref[3:4, :], 0.0))
    qkv_ref[...] = (contract(normed_ref[...], w_ref[...], ((1,), (0,))) + bias).astype(BF)


def resident(shape):
    return pl.BlockSpec(shape, lambda i, p: (0,) * len(shape), pipeline_mode=pl.Buffered(1))


def kept_half(rows):
    return pl.BlockSpec((1, rows, D), lambda i, p: (p[2], 0, 0), pipeline_mode=pl.Buffered(1))


def first(scalars, halves, got, vectors, blocks):
    half = halves.shape[1]
    rows = 2 * half
    across = lambda height: pl.BlockSpec((height, D), lambda i, p: (0, i))
    return pl.pallas_call(
        first_kernel,
        grid_spec=pltpu.PrefetchScalarGridSpec(
            num_scalar_prefetch=1,
            grid=(3,),
            in_specs=[kept_half(half), resident((half, D)), resident(vectors.shape)]
            + [across(D // 4)] * 4,
            out_specs=[across(rows), resident((D, rows)), resident((rows, D))],
            scratch_shapes=[pltpu.VMEM((rows, D), BF), pltpu.VMEM((D, D), BF)],
        ),
        out_shape=[sds((rows, 3 * D), BF), sds((D, rows), BF), sds((rows, D), BF)],
        cost_estimate=cost(6 * rows * D * D, 12 * rows * D + 6 * D * D, rows),
        compiler_params=pltpu.CompilerParams(vmem_limit_bytes=62 * MIB),
        name="norm_and_projections",
    )(scalars, halves, got, vectors, *blocks)


def by_head(rows):
    lane = lax.broadcasted_iota(jnp.int32, rows.shape, 1)
    zero = jnp.zeros_like(rows)
    return jnp.concatenate(
        [jnp.where(lane < HEAD_DIM, rows, zero), jnp.where(lane >= HEAD_DIM, rows, zero)], axis=0
    )


def own_rows(both, width):
    return jnp.concatenate([both[:HEAD_DIM, :width], both[HEAD_DIM:, width:]], axis=0)


def query_side(q_ref, hot_ref):
    hot = hot_ref[...]
    q = by_head(q_ref[...] * jnp.asarray(HEAD_DIM**-0.5, BF))
    return jnp.concatenate([q, jnp.concatenate([hot, hot], axis=0)], axis=1)


def attn_fwd_kernel(q_ref, k_ref, v_ref, hot_ref, far_ref, *rest):
    o_ref, lse_ref = rest[-2:]
    width = q_ref.shape[0]
    qs = query_side(q_ref, hot_ref)
    ks = jnp.concatenate([k_ref[...], far_ref[...]], axis=1)
    s = contract(ks, qs, ((1,), (1,)))
    top = jnp.max(s, axis=0, keepdims=True)
    e = jnp.exp(s - top)
    tot = jnp.sum(e, axis=0, keepdims=True)
    p = (e * (1.0 / tot)).astype(BF)
    o = contract(v_ref[...], p, ((0,), (0,)))
    o_ref[...] = own_rows(o, width).T.astype(BF)
    lse_ref[0] = top + jnp.log(tot)


def pair_cols(rows, at):
    return pl.BlockSpec((rows, LANES), lambda p: (0, at + p))


def attn_fwd(qkv, hot, far, at, count, before=()):
    rows = qkv.shape[0]
    return pl.pallas_call(
        attn_fwd_kernel,
        grid=(count,),
        in_specs=[
            pair_cols(rows, at),
            pair_cols(rows, PAIRS + at),
            pair_cols(rows, 2 * PAIRS + at),
            fixed((rows, LANES)),
            fixed((rows, LANES)),
        ]
        + [pl.BlockSpec(memory_space=pl.ANY)] * len(before),
        out_specs=[pair_cols(rows, at), pl.BlockSpec((1, 1, 2 * rows), lambda p: (at + p, 0, 0))],
        out_shape=[sds((rows, D), BF), sds((PAIRS, 1, 2 * rows), F32)],
        input_output_aliases={5 + i: i for i in range(len(before))},
        cost_estimate=cost(
            16 * rows * rows * LANES * count, 8 * rows * LANES * count, 2 * count * rows * rows
        ),
        compiler_params=pltpu.CompilerParams(vmem_limit_bytes=62 * MIB),
        name="attention_forward",
    )(qkv, qkv, qkv, hot, far, *before)


def attn_bwd_kernel(
    q_ref, k_ref, v_ref, do_ref, hot_ref, far_ref, lse_ref, *rest
):
    grad_ref = rest[-1]
    width = q_ref.shape[0]
    qs = query_side(q_ref, hot_ref)
    do = by_head(do_ref[...])
    keys = k_ref[...]
    ks = jnp.concatenate([keys, far_ref[...]], axis=1)
    s = contract(ks, qs, ((1,), (1,)))
    p = jnp.exp(s - lse_ref[0])
    dp = contract(v_ref[...], do, ((1,), (1,)))
    t = p * dp
    inner = jnp.sum(t, axis=0, keepdims=True)
    ds = (t - p * inner).astype(BF)
    grad_ref[2] = contract(p.astype(BF), do, ((1,), (0,))).astype(BF)
    grad_ref[1] = contract(ds, qs[:, :LANES], ((1,), (0,))).astype(BF)
    dq = own_rows(contract(keys, ds, ((0,), (0,))), width)
    grad_ref[0] = (dq * HEAD_DIM**-0.5).T.astype(BF)


def attn_bwd(qkv, dout, hot, far, lse, at, count, before=()):
    rows = qkv.shape[0]
    return pl.pallas_call(
        attn_bwd_kernel,
        grid=(count,),
        in_specs=[
            pair_cols(rows, at),
            pair_cols(rows, PAIRS + at),
            pair_cols(rows, 2 * PAIRS + at),
            pair_cols(rows, at),
            fixed((rows, LANES)),
            fixed((rows, LANES)),
            pl.BlockSpec((1, 1, 2 * rows), lambda p: (at + p, 0, 0)),
        ]
        + [pl.BlockSpec(memory_space=pl.ANY)] * len(before),
        out_specs=pl.BlockSpec((3, rows, LANES), lambda p: (0, 0, at + p)),
        out_shape=sds((3, rows, D), BF),
        input_output_aliases={7 + i: i for i in range(len(before))},
        cost_estimate=cost(
            10 * rows * rows * LANES * count * 4, 14 * rows * LANES * count, 2 * count * rows * rows
        ),
        compiler_params=pltpu.CompilerParams(vmem_limit_bytes=62 * MIB),
        name="attention_backward",
    )(qkv, qkv, qkv, dout, hot, far, lse, *before)


def middle_kernel(
    par_ref, tok_ref, attn_ref, gkept_ref, ggot_ref, wo0, wo1, wo2, wo3, vec_ref, wi_ref, ib_ref, wb0, wb1, wb2, wb3,
    out_ref, mid_ref, agrad_ref, keep_ref, send_ref, gwb_ref, gib_ref, small_ref,
    resid, normed, normed_t, out_acc, in_acc, g_ref, wo_ref, wb_all, arrived,
):
    i = pl.program_id(0)
    parity = par_ref[1]

    def fetch(k, block):
        rows = block.shape[0]
        at = pl.multiple_of((par_ref[0] ^ k) * rows, rows)
        return pltpu.make_async_copy(block, wb_all.at[pl.ds(at, rows)], arrived.at[k])

    @pl.when(i == 0)
    def _():
        for k, block in enumerate((wb0, wb1, wb2, wb3)):
            fetch(k, block).start()
        place(g_ref, (gkept_ref.at[0], ggot_ref), par_ref[2])
        place(wo_ref, (wo0, wo1, wo2, wo3), par_ref[0])
        r = tok_ref[...].astype(F32) + contract(attn_ref[...], wo_ref[...], ((1,), (0,))) + vec_ref[4:5, :]
        resid[...] = r
        n, _ = row_stats(r)
        x = (n * vec_ref[5:6, :] + vec_ref[6:7, :]).astype(BF)
        normed[...] = x
        normed_t[...] = x.T
        out_acc[...] = jnp.zeros_like(out_acc)
        in_acc[...] = jnp.zeros_like(in_acc)
        for k, block in enumerate((wb0, wb1, wb2, wb3)):
            fetch(k, block).wait()

    x = normed[...]
    g = g_ref[...]
    wi = wi_ref[...]
    wb = wb_all[pl.ds(pl.multiple_of(i * HB, HB), HB), :]
    pre = contract(x, wi, ((1,), (0,))) + ib_ref[...]
    cdf = 0.5 + 0.5 * lax.erf(pre * 0.7071067811865476)
    h = (pre * cdf).astype(BF)
    slope = cdf + pre * (0.3989422804014327 * jnp.exp(-0.5 * (pre * pre)))
    pg = (contract(g, wb, ((1,), (1,))) * slope).astype(BF)
    out_acc[...] += contract(h, wb, ((1,), (0,)))
    in_acc[...] += contract(pg, wi, ((1,), (1,)))
    at = pl.multiple_of(i * HB, HB)
    put_parities(contract(normed_t[...], pg, ((1,), (0,))), parity, keep_ref, send_ref, at)
    gwb_ref[...] = contract(h, g, ((0,), (0,))).astype(BF)
    gib_ref[...] = jnp.sum(pg.astype(F32), axis=0, keepdims=True)

    @pl.when(i == pl.num_programs(0) - 1)
    def _():
        r = resid[...]
        out_ref[...] = (r + out_acc[...] + vec_ref[7:8, :]).astype(BF)
        n, rstd = row_stats(r)
        d = in_acc[...]
        gf = g_ref[...].astype(F32)
        m = gf + norm_back(d, n, rstd, vec_ref[5:6, :])
        mid_ref[...] = m
        b = m.astype(BF)
        small_ref[0:1, :] = jnp.sum(b.astype(F32), axis=0, keepdims=True)
        small_ref[1:2, :] = jnp.sum(d * n, axis=0, keepdims=True)
        small_ref[2:3, :] = jnp.sum(d, axis=0, keepdims=True)
        small_ref[3:4, :] = jnp.sum(gf, axis=0, keepdims=True)
        agrad_ref[...] = contract(b, wo_ref[...], ((1,), (1,))).astype(BF)
        put_parities(
            contract(attn_ref[...], b, ((0,), (0,))), parity, keep_ref, send_ref,
            keep_ref.shape[2] - D,
        )


def middle(scalars, tokens, attn, halves, got, w_out, vectors, w_in, in_bias, w_back):
    rows = tokens.shape[0]
    ff = w_in.shape[1]
    shards = lax.axis_size("shard")
    half = (shards // 2, D // shards, ff + D)
    return pl.pallas_call(
        middle_kernel,
        grid_spec=pltpu.PrefetchScalarGridSpec(
            num_scalar_prefetch=1,
            grid=(ff // HB,),
            in_specs=[
                resident((rows, D)),
                resident((rows, D)),
                kept_half(rows // 2),
                resident((rows // 2, D)),
            ]
            + [resident((D // 4, D))] * 4
            + [resident(vectors.shape)]
            + [
                pl.BlockSpec((D, HB), lambda i, p: (0, i)),
                pl.BlockSpec((1, HB), lambda i, p: (0, i)),
            ]
            + [pl.BlockSpec(memory_space=pl.ANY)] * 4,
            out_specs=[
                resident((rows, D)),
                resident((rows, D)),
                resident((rows, D)),
                resident(half),
                resident(half),
                pl.BlockSpec((HB, D), lambda i, p: (i, 0)),
                pl.BlockSpec((1, HB), lambda i, p: (0, i)),
                resident((8, D)),
            ],
            scratch_shapes=[
                pltpu.VMEM((rows, D), F32),
                pltpu.VMEM((rows, D), BF),
                pltpu.VMEM((D, rows), BF),
                pltpu.VMEM((rows, D), F32),
                pltpu.VMEM((rows, D), F32),
                pltpu.VMEM((rows, D), BF),
                pltpu.VMEM((D, D), BF),
                pltpu.VMEM((ff, D), BF),
                pltpu.SemaphoreType.DMA((4,)),
            ],
        ),
        out_shape=[
            sds((rows, D), BF),
            sds((rows, D), F32),
            sds((rows, D), BF),
            sds(half, BF),
            sds(half, BF),
            sds((ff, D), BF),
            sds((1, ff), F32),
            sds((8, D), F32),
        ],
        cost_estimate=cost(2 * rows * D * (6 * ff + 3 * D), 10 * D * ff + 20 * rows * D, 2 * rows * ff),
        compiler_params=pltpu.CompilerParams(vmem_limit_bytes=62 * MIB),
        name="projection_and_feed_forward",
    )(scalars, tokens, attn, halves, got, *w_out, vectors, w_in, in_bias, *w_back)


def last_kernel(
    pos_ref, turned_ref, tok_ref, mid_ref, vec_ref, small_ref, gib_ref, d_ref, w0, w1, w2, w3,
    tgrad_ref, keep_ref, send_ref, total, columns, w_ref,
):
    i = pl.program_id(0)
    parity = pos_ref[1]
    d = d_ref[0]

    @pl.when(i == 0)
    def _():
        columns[...] = jnp.zeros_like(columns)
        columns[4:8, :] = small_ref[0:4, :]
        columns[8 : 8 + gib_ref.shape[0], :] = gib_ref[...]
        total[...] = jnp.zeros_like(total)
        columns[2:3, :] = jnp.sum(d.astype(F32), axis=0, keepdims=True)

    at = pl.multiple_of(i * D, D)
    put_parities(contract(turned_ref[...], d, ((1,), (0,))), parity, keep_ref, send_ref, at)
    place(w_ref, (w0, w1, w2, w3), pos_ref[0])
    total[...] += contract(d, w_ref[...], ((1,), (1,)))

    @pl.when(i == 2)
    def _():
        columns[3:4, :] = jnp.sum(d.astype(F32), axis=0, keepdims=True)
        t = total[...]
        n, rstd = row_stats(tok_ref[...].astype(F32))
        tgrad_ref[...] = (mid_ref[...] + norm_back(t, n, rstd, vec_ref[0:1, :])).astype(BF)
        columns[0:1, :] = jnp.sum(t * n, axis=0, keepdims=True)
        columns[1:2, :] = jnp.sum(t, axis=0, keepdims=True)
        put_parities(columns[...].T, parity, keep_ref, send_ref, 3 * D)


def last(scalars, turned, tokens, mid_grad, vectors, small, g_inb, grads, blocks):
    rows = tokens.shape[0]
    shards = lax.axis_size("shard")
    half = (shards // 2, D // shards, 3 * D + LANES)
    return pl.pallas_call(
        last_kernel,
        grid_spec=pltpu.PrefetchScalarGridSpec(
            num_scalar_prefetch=1,
            grid=(3,),
            in_specs=[
                resident((D, rows)),
                resident((rows, D)),
                resident((rows, D)),
                resident(vectors.shape),
                resident((8, D)),
                resident(g_inb.shape),
                pl.BlockSpec((1, rows, D), lambda i, p: (i, 0, 0)),
            ]
            + [pl.BlockSpec((D // 4, D), lambda i, p: (0, i))] * 4,
            out_specs=[resident((rows, D)), resident(half), resident(half)],
            scratch_shapes=[
                pltpu.VMEM((rows, D), F32),
                pltpu.VMEM((LANES, D), F32),
                pltpu.VMEM((D, D), BF),
            ],
        ),
        out_shape=[sds((rows, D), BF), sds(half, BF), sds(half, BF)],
        cost_estimate=cost(12 * rows * D * D, 20 * rows * D + 12 * D * D, rows),
        compiler_params=pltpu.CompilerParams(vmem_limit_bytes=62 * MIB),
        name="projections_backward",
    )(scalars, turned, tokens, mid_grad, vectors, small, g_inb, grads, *blocks)


def by_shard(vector):
    shards = lax.axis_size("shard")
    count = vector.shape[1] // D
    return vector.reshape(shards, count, D // shards).transpose(1, 0, 2).reshape(count, D)


def layer(shards, vec, halves, ids, out_halves):
    qkv_shard, out_shard, in_shard, back_shard = shards
    me = lax.axis_index("seq").astype(jnp.int32)
    count = lax.axis_size("shard")
    mine = lax.axis_index("shard").astype(jnp.int32)
    near, far_axis = bits("seq")[0], bits("rep")
    direct = count == 4
    position = mine if direct else jnp.int32(0)
    scalars = jnp.stack([position, mine % 2, me])
    gather = lambda w: lax.all_gather(w, "shard", axis=0, tiled=True)
    to_core = lambda w: xor_send(w, "shard", 1)

    got_tokens = xor_send(pick(halves, 1 - me), "seq", 1)
    if direct:
        split = part_axes(back_shard)
        vec = vec.reshape(1, -1)
        across, vec_across = xor_send(qkv_shard, "shard", 2), xor_send(vec, "shard", 2)
        beside, vec_beside = to_core(qkv_shard), to_core(vec)
        across, vec_across, got_tokens, out_shard, in_shard, back_shard = tie(
            across, vec_across, got_tokens, out_shard, in_shard, back_shard
        )
        w_qkv = [qkv_shard, beside, across, to_core(across)]
        back_piece = fetch_part(back_shard, split)
        out_across = xor_send(out_shard, "shard", 2)
        out_beside, back_beside = to_core(out_shard), to_core(back_shard)
        near_two = jnp.concatenate([vec, vec_beside]).astype(F32)
        far_two = jnp.concatenate([vec_across, to_core(vec_across)]).astype(F32)
        odd, high = position % 2 == 1, position >= 2
        near_two = jnp.where(odd, near_two[::-1], near_two)
        far_two = jnp.where(odd, far_two[::-1], far_two)
        vec_all = jnp.where(
            high, jnp.concatenate([far_two, near_two]), jnp.concatenate([near_two, far_two])
        )
    else:
        w_qkv = quarters(gather(qkv_shard))
        vec_all = lax.all_gather(vec, "shard", axis=0).astype(F32)
    cell = D // count
    vectors = vec_all[:, : 8 * cell].reshape(count, 8, cell).transpose(1, 0, 2).reshape(8, D)
    in_bias = vec_all[:, 8 * cell :].reshape(1, -1)
    qkv, turned, tokens = first(scalars, halves, got_tokens, vectors, w_qkv)
    qkv, in_shard = tie(qkv, in_shard)
    w_in = gather(in_shard)
    same = ids[:, None] == jnp.arange(LANES, dtype=ids.dtype)[None, :]
    hot = same.astype(BF)
    far = jnp.where(same, 0.0, FAR).astype(BF)
    if direct:
        qkv, back_piece = tie(qkv, back_piece)
    for step in reversed(split[1:] if direct else []):
        back_piece = join(back_piece, step, 0)
    attn = attn_fwd(qkv, hot, far, 0, PAIRS // 2)
    *attn, out_halves = tie(*attn, out_halves)
    got_grad = xor_send(pick(out_halves, 1 - me), "seq", 1)
    if direct:
        *attn, back_piece, out_across = tie(*attn, back_piece, out_across)
        back_piece = join(back_piece, split[0], 0)
        w_out = [out_shard, out_beside, out_across, to_core(out_across)]
    attn, lse = attn_fwd(qkv, hot, far, PAIRS // 2, PAIRS - PAIRS // 2, attn)
    attn, got_grad, w_in = tie(attn, got_grad, w_in)
    if direct:
        attn, back_piece, w_out[3] = tie(attn, back_piece, w_out[3])
        w_back = [back_shard, back_beside, back_piece, to_core(back_piece)]
    else:
        w_out = quarters(gather(out_shard))
        w_back = quarters(gather(back_shard))
    block_out, mid_grad, attn_grad, keep, send, g_wback, g_inb, small = middle(
        scalars, tokens, attn, out_halves, got_grad, w_out, vectors, w_in, in_bias, w_back
    )
    s = lax.psum_scatter(g_wback, "shard", scatter_dimension=0, tiled=True)[None]
    got = to_core(send)
    block_out = block_out.reshape(halves.shape)
    got_out = xor_send(pick(block_out, 1 - me), "seq", 1)
    grads = attn_bwd(qkv, attn_grad, hot, far, lse, 0, SPLIT)
    grads, got = tie(grads, got)
    first_far, rest_far = far_axis[0], far_axis[1:]
    by_axis = lambda v: v.reshape(v.shape[0], 2, 2, v.shape[1] // 4, v.shape[2])
    f = [by_axis(v) for v in (keep, got)]
    wide = f[0].shape[4]
    middle_col = LANES * (wide // (2 * LANES))
    f1 = halve([v[..., :middle_col] for v in f], near, 1)
    f2 = halve([v[..., middle_col:] for v in f], first_far, 2)
    grads = attn_bwd(qkv, attn_grad, hot, far, lse, SPLIT, PAIRS - SPLIT, [grads])
    grads, got_out, s, f1, f2 = tie(grads, got_out, s, f1, f2)
    f1, f2 = halve(f1, first_far, 2), halve(f2, near, 1)
    s = halve((s, jnp.zeros_like(s)), near, 1)
    token_grad, keep, send = last(
        scalars, turned, tokens, mid_grad, vectors, small, by_shard(g_inb), grads, w_qkv
    )

    token_grad, send, f1, f2, s = tie(token_grad, send, f1, f2, s)
    t = (keep, to_core(send))
    f = chips([jnp.concatenate([v, w], axis=4) for v, w in zip(f1, f2)])
    s = halve(s, first_far, 1)
    t, f, s, token_grad = tie(t, f, s, token_grad)
    t = chips(t)
    token_grad = token_grad.reshape(halves.shape)
    got_tokens = xor_send(pick(token_grad, 1 - me), "seq", 1)
    f = last_steps(f, rest_far)
    t, f, got_tokens = tie(t, f, got_tokens)
    t = halve(t, near, 1)
    s = last_steps(s, rest_far)
    f = join(f, first_far, 2)
    t, f = tie(t, f)
    t = halve(t, first_far, 1)
    f = join(f, near, 1)
    t, s = tie(t, s)
    t = last_steps(t, rest_far)
    s = join(s, first_far, 1)
    t, f, s = tie(t, f, s)
    t = join(t, first_far, 1)
    s = join(s, near, 1)
    t, s = tie(t, s)
    t = join(t, near, 1)
    outputs = [
        jnp.stack([jnp.where(me == 0, kept, got), jnp.where(me == 0, got, kept)])
        for kept, got in ((pick(block_out, me), got_out), (pick(token_grad, me), got_tokens))
    ]
    flat = lambda v: v[0].reshape(-1, v.shape[-1]).astype(F32)
    return outputs[0], outputs[1], [s[0].astype(F32), flat(f), flat(t)]


def last_steps(state, order):
    for step in order:
        state = whole(state, step)
    return added(state)


def body(
    tokens,
    segment_ids,
    out_grad,
    norm1_gain,
    norm1_bias,
    qkv_weight,
    query_bias,
    value_bias,
    out_weight,
    out_bias,
    norm2_gain,
    norm2_bias,
    ff_in_weight,
    ff_in_bias,
    ff_out_weight,
    ff_out_bias,
):
    seqs, row_count, _ = tokens.shape
    ways = lax.axis_size("seq")
    me = lax.axis_index("seq")
    wide = ff_in_weight.shape[1]

    vec = jnp.concatenate(
        [
            norm1_gain,
            norm1_bias,
            query_bias,
            value_bias,
            out_bias,
            norm2_gain,
            norm2_bias,
            ff_out_bias,
            ff_in_bias,
        ]
    )
    weights = (qkv_weight, out_weight, ff_in_weight, ff_out_weight)

    out_parts, grad_parts, sums = [], [], None
    for lo in range(0, seqs, ways):
        ids = pick(segment_ids[lo : lo + ways], me)
        block, tgrad, terms = layer(
            weights, vec, tokens[lo : lo + ways], ids, out_grad[lo : lo + ways]
        )
        out_parts.append(block)
        grad_parts.append(tgrad)
        sums = terms if sums is None else [a + b for a, b in zip(sums, terms)]
    g_wback, g_in, g_t = sums
    small = g_t[:, 3 * D : 3 * D + 8 + g_in.shape[1] // D - 1].T
    return (
        jnp.concatenate(out_parts, axis=0),
        jnp.concatenate(grad_parts, axis=0),
        small[0],
        small[1],
        g_t[:, : 3 * D],
        small[2],
        small[3],
        g_in[:, wide:],
        small[4],
        small[5],
        small[6],
        g_in[:, :wide],
        small[8:].reshape(-1),
        g_wback,
        small[7],
    )


def solution(mesh):
    in_specs = (
        P(("shard", "rep"), "seq", None),
        P(("shard", "rep"), None),
        P(("shard", "rep"), "seq", None),
        P("shard"),
        P("shard"),
        P("shard", None),
        P("shard"),
        P("shard"),
        P("shard", None),
        P("shard"),
        P("shard"),
        P("shard"),
        P("shard", None),
        P("shard"),
        P("shard", None),
        P("shard"),
    )
    out_specs = (
        P(("shard", "rep"), "seq", None),
        P(("shard", "rep"), "seq", None),
        P("shard"),
        P("shard"),
        P("shard", None),
        P("shard"),
        P("shard"),
        P("shard", None),
        P("shard"),
        P("shard"),
        P("shard"),
        P("shard", None),
        P("shard"),
        P("shard", None),
        P("shard"),
    )
    return jax.shard_map(body, mesh=mesh, in_specs=in_specs, out_specs=out_specs, check_vma=False)
```

```python
import jax
import jax.numpy as jnp
from jax import lax
from jax.experimental import pallas as pl
from jax.experimental.pallas import tpu as pltpu
from jax.sharding import PartitionSpec as P

D = 768
HEADS = 12
HEAD_DIM = 64
LANES = 128
HB = 512
SPLIT = 2
PAIRS = HEADS // 2
FAR = -1e30
BF = jnp.bfloat16
F32 = jnp.float32
MIB = 1 << 20


def xor_send(value, axis, mask):
    size = lax.axis_size(axis)
    return lax.ppermute(value, axis, [(i, i ^ mask) for i in range(size)])


def bits(axis):
    return [(axis, 1 << b) for b in range((lax.axis_size(axis) - 1).bit_length())]


def bit_of(axis, mask):
    return (lax.axis_index(axis) // mask) % 2


def pick(stacked, index):
    return lax.dynamic_index_in_dim(stacked, index, 0, keepdims=False)


def tie(*values):
    return lax.optimization_barrier(values)


def added(state):
    return (state[0].astype(F32) + state[1].astype(F32)).astype(state[0].dtype)


def cut_half(state, step, dim):
    bit = bit_of(*step)
    size = state[0].shape[dim] // 2
    cut = lambda at: added([lax.dynamic_slice_in_dim(s, at * size, size, dim) for s in state])
    return cut(bit), cut(1 - bit)


def send_half(parts, step):
    return parts[0], xor_send(parts[1], *step)


def halve(state, step, dim):
    return send_half(cut_half(state, step, dim), step)


def whole(state, step):
    value = added(state)
    return value, xor_send(value, *step)


def join(part, step, dim):
    bit = bit_of(*step)
    other = xor_send(part, *step)
    low = jnp.where(bit == 0, part, other)
    high = jnp.where(bit == 0, other, part)
    return jnp.concatenate([low, high], axis=dim)


def cut_chips(state, mask):
    bit = bit_of("shard", mask)

    def cut(at):
        split = [s.reshape((s.shape[0] // 2, 2) + s.shape[1:]) for s in state]
        return added([lax.dynamic_index_in_dim(s, at, 1, keepdims=False) for s in split])

    return cut(bit), cut(1 - bit)


def chips(state, mask=2):
    while mask < lax.axis_size("shard"):
        state = send_half(cut_chips(state, mask), ("shard", mask))
        mask *= 2
    return state


def quarters(full):
    rows = full.shape[0] // 4
    return [full[k * rows : (k + 1) * rows] for k in range(4)]


def part_axes(shard):
    parts = bits("rep")[:1] + bits("seq")
    return parts if shard.shape[0] % (8 << len(parts)) == 0 else []


def fetch_part(shard, parts):
    piece = shard
    for axis, mask in parts:
        half = piece.shape[0] // 2
        piece = lax.dynamic_slice_in_dim(piece, bit_of(axis, mask) * half, half)
    return xor_send(piece, "shard", 2)


def cost(flops, bytes_accessed, transcendentals):
    return pl.CostEstimate(
        flops=flops, bytes_accessed=bytes_accessed, transcendentals=transcendentals
    )


def sds(shape, dtype):
    return jax.ShapeDtypeStruct(shape, dtype)


def fixed(shape):
    return pl.BlockSpec(shape, lambda i: (0,) * len(shape), pipeline_mode=pl.Buffered(1))


def contract(left, right, dims):
    return lax.dot_general(left, right, (dims, ((), ())), preferred_element_type=F32)


def row_stats(rows):
    mean = jnp.mean(rows, axis=-1, keepdims=True)
    centered = rows - mean
    rstd = lax.rsqrt(jnp.mean(centered * centered, axis=-1, keepdims=True) + 1e-06)
    return centered * rstd, rstd


def norm_back(in_grad, normal, rstd, gain):
    scaled = in_grad * gain
    mean_e = jnp.mean(scaled, axis=-1, keepdims=True)
    mean_en = jnp.mean(scaled * normal, axis=-1, keepdims=True)
    return rstd * (scaled - mean_e - normal * mean_en)


def put_parities(value, parity, keep_ref, send_ref, at):
    blocks, rows = keep_ref.shape[0], keep_ref.shape[1]
    cols = pl.ds(at, value.shape[1])
    for k in range(blocks):
        even = value[2 * k * rows : (2 * k + 1) * rows]
        odd = value[(2 * k + 1) * rows : (2 * k + 2) * rows]
        keep_ref[k, :, cols] = jnp.where(parity == 0, even, odd).astype(keep_ref.dtype)
        send_ref[k, :, cols] = jnp.where(parity == 0, odd, even).astype(send_ref.dtype)


def place(ref, blocks, position):
    rows = blocks[0].shape[0]
    for k, block in enumerate(blocks):
        at = pl.multiple_of((position ^ k) * rows, rows)
        ref[pl.ds(at, rows), :] = block[...]


def first_kernel(pos_ref, kept_ref, got_ref, vec_ref, w0, w1, w2, w3, qkv_ref, turned_ref, tok_ref, normed_ref, w_ref):
    i = pl.program_id(0)

    @pl.when(i == 0)
    def _():
        place(tok_ref, (kept_ref.at[0], got_ref), pos_ref[2])
        n, _ = row_stats(tok_ref[...].astype(F32))
        x = (n * vec_ref[0:1, :] + vec_ref[1:2, :]).astype(BF)
        normed_ref[...] = x
        turned_ref[...] = x.T

    place(w_ref, (w0, w1, w2, w3), pos_ref[0])
    bias = jnp.where(i == 0, vec_ref[2:3, :], jnp.where(i == 2, vec_ref[3:4, :], 0.0))
    qkv_ref[...] = (contract(normed_ref[...], w_ref[...], ((1,), (0,))) + bias).astype(BF)


def resident(shape):
    return pl.BlockSpec(shape, lambda i, p: (0,) * len(shape), pipeline_mode=pl.Buffered(1))


def kept_half(rows):
    return pl.BlockSpec((1, rows, D), lambda i, p: (p[2], 0, 0), pipeline_mode=pl.Buffered(1))


def first(scalars, halves, got, vectors, blocks):
    half = halves.shape[1]
    rows = 2 * half
    across = lambda height: pl.BlockSpec((height, D), lambda i, p: (0, i))
    return pl.pallas_call(
        first_kernel,
        grid_spec=pltpu.PrefetchScalarGridSpec(
            num_scalar_prefetch=1,
            grid=(3,),
            in_specs=[kept_half(half), resident((half, D)), resident(vectors.shape)]
            + [across(D // 4)] * 4,
            out_specs=[across(rows), resident((D, rows)), resident((rows, D))],
            scratch_shapes=[pltpu.VMEM((rows, D), BF), pltpu.VMEM((D, D), BF)],
        ),
        out_shape=[sds((rows, 3 * D), BF), sds((D, rows), BF), sds((rows, D), BF)],
        cost_estimate=cost(6 * rows * D * D, 12 * rows * D + 6 * D * D, rows),
        compiler_params=pltpu.CompilerParams(vmem_limit_bytes=62 * MIB),
        name="norm_and_projections",
    )(scalars, halves, got, vectors, *blocks)


def by_head(rows):
    lane = lax.broadcasted_iota(jnp.int32, rows.shape, 1)
    zero = jnp.zeros_like(rows)
    return jnp.concatenate(
        [jnp.where(lane < HEAD_DIM, rows, zero), jnp.where(lane >= HEAD_DIM, rows, zero)], axis=0
    )


def own_rows(both, width):
    return jnp.concatenate([both[:HEAD_DIM, :width], both[HEAD_DIM:, width:]], axis=0)


def query_side(q_ref, hot_ref):
    hot = hot_ref[...]
    q = by_head(q_ref[...] * jnp.asarray(HEAD_DIM**-0.5, BF))
    return jnp.concatenate([q, jnp.concatenate([hot, hot], axis=0)], axis=1)


def attn_fwd_kernel(q_ref, k_ref, v_ref, hot_ref, far_ref, *rest):
    o_ref, lse_ref = rest[-2:]
    width = q_ref.shape[0]
    qs = query_side(q_ref, hot_ref)
    ks = jnp.concatenate([k_ref[...], far_ref[...]], axis=1)
    s = contract(ks, qs, ((1,), (1,)))
    top = jnp.max(s, axis=0, keepdims=True)
    e = jnp.exp(s - top)
    tot = jnp.sum(e, axis=0, keepdims=True)
    p = (e * (1.0 / tot)).astype(BF)
    o = contract(v_ref[...], p, ((0,), (0,)))
    o_ref[...] = own_rows(o, width).T.astype(BF)
    lse_ref[0] = top + jnp.log(tot)


def pair_cols(rows, at):
    return pl.BlockSpec((rows, LANES), lambda p: (0, at + p))


def attn_fwd(qkv, hot, far, at, count, before=()):
    rows = qkv.shape[0]
    return pl.pallas_call(
        attn_fwd_kernel,
        grid=(count,),
        in_specs=[
            pair_cols(rows, at),
            pair_cols(rows, PAIRS + at),
            pair_cols(rows, 2 * PAIRS + at),
            fixed((rows, LANES)),
            fixed((rows, LANES)),
        ]
        + [pl.BlockSpec(memory_space=pl.ANY)] * len(before),
        out_specs=[pair_cols(rows, at), pl.BlockSpec((1, 1, 2 * rows), lambda p: (at + p, 0, 0))],
        out_shape=[sds((rows, D), BF), sds((PAIRS, 1, 2 * rows), F32)],
        input_output_aliases={5 + i: i for i in range(len(before))},
        cost_estimate=cost(
            16 * rows * rows * LANES * count, 8 * rows * LANES * count, 2 * count * rows * rows
        ),
        compiler_params=pltpu.CompilerParams(vmem_limit_bytes=62 * MIB),
        name="attention_forward",
    )(qkv, qkv, qkv, hot, far, *before)


def attn_bwd_kernel(
    q_ref, k_ref, v_ref, do_ref, hot_ref, far_ref, lse_ref, *rest
):
    grad_ref = rest[-1]
    width = q_ref.shape[0]
    qs = query_side(q_ref, hot_ref)
    do = by_head(do_ref[...])
    keys = k_ref[...]
    ks = jnp.concatenate([keys, far_ref[...]], axis=1)
    s = contract(ks, qs, ((1,), (1,)))
    p = jnp.exp(s - lse_ref[0])
    dp = contract(v_ref[...], do, ((1,), (1,)))
    t = p * dp
    inner = jnp.sum(t, axis=0, keepdims=True)
    ds = (t - p * inner).astype(BF)
    grad_ref[2] = contract(p.astype(BF), do, ((1,), (0,))).astype(BF)
    grad_ref[1] = contract(ds, qs[:, :LANES], ((1,), (0,))).astype(BF)
    dq = own_rows(contract(keys, ds, ((0,), (0,))), width)
    grad_ref[0] = (dq * HEAD_DIM**-0.5).T.astype(BF)


def attn_bwd(qkv, dout, hot, far, lse, at, count, before=()):
    rows = qkv.shape[0]
    return pl.pallas_call(
        attn_bwd_kernel,
        grid=(count,),
        in_specs=[
            pair_cols(rows, at),
            pair_cols(rows, PAIRS + at),
            pair_cols(rows, 2 * PAIRS + at),
            pair_cols(rows, at),
            fixed((rows, LANES)),
            fixed((rows, LANES)),
            pl.BlockSpec((1, 1, 2 * rows), lambda p: (at + p, 0, 0)),
        ]
        + [pl.BlockSpec(memory_space=pl.ANY)] * len(before),
        out_specs=pl.BlockSpec((3, rows, LANES), lambda p: (0, 0, at + p)),
        out_shape=sds((3, rows, D), BF),
        input_output_aliases={7 + i: i for i in range(len(before))},
        cost_estimate=cost(
            10 * rows * rows * LANES * count * 4, 14 * rows * LANES * count, 2 * count * rows * rows
        ),
        compiler_params=pltpu.CompilerParams(vmem_limit_bytes=62 * MIB),
        name="attention_backward",
    )(qkv, qkv, qkv, dout, hot, far, lse, *before)


def put_halves(rows, mine, own_ref, other_ref):
    half = own_ref.shape[0]
    low, high = rows[:half], rows[half:]
    own_ref[...] = jnp.where(mine == 0, low, high)
    other_ref[...] = jnp.where(mine == 0, high, low)


def middle_kernel(
    par_ref, tok_ref, attn_ref, gkept_ref, ggot_ref, wo0, wo1, wo2, wo3, vec_ref, wi_ref, ib_ref, wb0, wb1, wb2, wb3,
    own_ref, other_ref, mid_ref, agrad_ref, keep_ref, send_ref, gwb_ref, gib_ref, small_ref,
    resid, normed, normed_t, out_acc, in_acc, g_ref, wo_ref, wb_all, arrived,
):
    i = pl.program_id(0)
    parity = par_ref[1]

    def fetch(k, block):
        rows = block.shape[0]
        at = pl.multiple_of((par_ref[0] ^ k) * rows, rows)
        return pltpu.make_async_copy(block, wb_all.at[pl.ds(at, rows)], arrived.at[k])

    @pl.when(i == 0)
    def _():
        for k, block in enumerate((wb0, wb1, wb2, wb3)):
            fetch(k, block).start()
        place(g_ref, (gkept_ref.at[0], ggot_ref), par_ref[2])
        place(wo_ref, (wo0, wo1, wo2, wo3), par_ref[0])
        r = tok_ref[...].astype(F32) + contract(attn_ref[...], wo_ref[...], ((1,), (0,))) + vec_ref[4:5, :]
        resid[...] = r
        n, _ = row_stats(r)
        x = (n * vec_ref[5:6, :] + vec_ref[6:7, :]).astype(BF)
        normed[...] = x
        normed_t[...] = x.T
        out_acc[...] = jnp.zeros_like(out_acc)
        in_acc[...] = jnp.zeros_like(in_acc)
        for k, block in enumerate((wb0, wb1, wb2, wb3)):
            fetch(k, block).wait()

    x = normed[...]
    g = g_ref[...]
    wi = wi_ref[...]
    wb = wb_all[pl.ds(pl.multiple_of(i * HB, HB), HB), :]
    pre = contract(x, wi, ((1,), (0,))) + ib_ref[...]
    cdf = 0.5 + 0.5 * lax.erf(pre * 0.7071067811865476)
    h = (pre * cdf).astype(BF)
    slope = cdf + pre * (0.3989422804014327 * jnp.exp(-0.5 * (pre * pre)))
    pg = (contract(g, wb, ((1,), (1,))) * slope).astype(BF)
    out_acc[...] += contract(h, wb, ((1,), (0,)))
    in_acc[...] += contract(pg, wi, ((1,), (1,)))
    at = pl.multiple_of(i * HB, HB)
    put_parities(contract(normed_t[...], pg, ((1,), (0,))), parity, keep_ref, send_ref, at)
    gwb_ref[...] = contract(h, g, ((0,), (0,))).astype(BF)
    gib_ref[...] = jnp.sum(pg.astype(F32), axis=0, keepdims=True)

    @pl.when(i == pl.num_programs(0) - 1)
    def _():
        r = resid[...]
        put_halves((r + out_acc[...] + vec_ref[7:8, :]).astype(BF), par_ref[2], own_ref, other_ref)
        n, rstd = row_stats(r)
        d = in_acc[...]
        gf = g_ref[...].astype(F32)
        m = gf + norm_back(d, n, rstd, vec_ref[5:6, :])
        mid_ref[...] = m
        b = m.astype(BF)
        small_ref[0:1, :] = jnp.sum(b.astype(F32), axis=0, keepdims=True)
        small_ref[1:2, :] = jnp.sum(d * n, axis=0, keepdims=True)
        small_ref[2:3, :] = jnp.sum(d, axis=0, keepdims=True)
        small_ref[3:4, :] = jnp.sum(gf, axis=0, keepdims=True)
        agrad_ref[...] = contract(b, wo_ref[...], ((1,), (1,))).astype(BF)
        put_parities(
            contract(attn_ref[...], b, ((0,), (0,))), parity, keep_ref, send_ref,
            keep_ref.shape[2] - D,
        )


def middle(scalars, tokens, attn, halves, got, w_out, vectors, w_in, in_bias, w_back):
    rows = tokens.shape[0]
    ff = w_in.shape[1]
    shards = lax.axis_size("shard")
    half = (shards // 2, D // shards, ff + D)
    return pl.pallas_call(
        middle_kernel,
        grid_spec=pltpu.PrefetchScalarGridSpec(
            num_scalar_prefetch=1,
            grid=(ff // HB,),
            in_specs=[
                resident((rows, D)),
                resident((rows, D)),
                kept_half(rows // 2),
                resident((rows // 2, D)),
            ]
            + [resident((D // 4, D))] * 4
            + [resident(vectors.shape)]
            + [
                pl.BlockSpec((D, HB), lambda i, p: (0, i)),
                pl.BlockSpec((1, HB), lambda i, p: (0, i)),
            ]
            + [pl.BlockSpec(memory_space=pl.ANY)] * 4,
            out_specs=[
                resident((rows // 2, D)),
                resident((rows // 2, D)),
                resident((rows, D)),
                resident((rows, D)),
                resident(half),
                resident(half),
                pl.BlockSpec((HB, D), lambda i, p: (i, 0)),
                pl.BlockSpec((1, HB), lambda i, p: (0, i)),
                resident((8, D)),
            ],
            scratch_shapes=[
                pltpu.VMEM((rows, D), F32),
                pltpu.VMEM((rows, D), BF),
                pltpu.VMEM((D, rows), BF),
                pltpu.VMEM((rows, D), F32),
                pltpu.VMEM((rows, D), F32),
                pltpu.VMEM((rows, D), BF),
                pltpu.VMEM((D, D), BF),
                pltpu.VMEM((ff, D), BF),
                pltpu.SemaphoreType.DMA((4,)),
            ],
        ),
        out_shape=[
            sds((rows // 2, D), BF),
            sds((rows // 2, D), BF),
            sds((rows, D), F32),
            sds((rows, D), BF),
            sds(half, BF),
            sds(half, BF),
            sds((ff, D), BF),
            sds((1, ff), F32),
            sds((8, D), F32),
        ],
        cost_estimate=cost(2 * rows * D * (6 * ff + 3 * D), 10 * D * ff + 20 * rows * D, 2 * rows * ff),
        compiler_params=pltpu.CompilerParams(vmem_limit_bytes=62 * MIB),
        name="projection_and_feed_forward",
    )(scalars, tokens, attn, halves, got, *w_out, vectors, w_in, in_bias, *w_back)


def last_kernel(
    pos_ref, tok_ref, mid_ref, vec_ref, small_ref, gib_ref, d_ref, w0, w1, w2, w3,
    own_ref, other1_ref, other2_ref, columns, total, w_ref,
):
    i = pl.program_id(0)
    d = d_ref[0]

    @pl.when(i == 0)
    def _():
        columns[...] = jnp.zeros_like(columns)
        columns[4:8, :] = small_ref[0:4, :]
        columns[8 : 8 + gib_ref.shape[0], :] = gib_ref[...]
        total[...] = jnp.zeros_like(total)
        columns[2:3, :] = jnp.sum(d.astype(F32), axis=0, keepdims=True)

    place(w_ref, (w0, w1, w2, w3), pos_ref[0])
    total[...] += contract(d, w_ref[...], ((1,), (1,)))

    @pl.when(i == 2)
    def _():
        columns[3:4, :] = jnp.sum(d.astype(F32), axis=0, keepdims=True)
        t = total[...]
        n, rstd = row_stats(tok_ref[...].astype(F32))
        token_grad = (mid_ref[...] + norm_back(t, n, rstd, vec_ref[0:1, :])).astype(BF)
        half = own_ref.shape[0]
        low, high = token_grad[:half], token_grad[half:]
        own_ref[...] = jnp.where(pos_ref[2] == 0, low, high)
        other = jnp.where(pos_ref[2] == 0, high, low)
        other1_ref[...] = other[: half // 2]
        other2_ref[...] = other[half // 2 :]
        columns[0:1, :] = jnp.sum(t * n, axis=0, keepdims=True)
        columns[1:2, :] = jnp.sum(t, axis=0, keepdims=True)


def last(scalars, tokens, mid_grad, vectors, small, g_inb, grads, blocks):
    rows = tokens.shape[0]
    return pl.pallas_call(
        last_kernel,
        grid_spec=pltpu.PrefetchScalarGridSpec(
            num_scalar_prefetch=1,
            grid=(3,),
            in_specs=[
                resident((rows, D)),
                resident((rows, D)),
                resident(vectors.shape),
                resident((8, D)),
                resident(g_inb.shape),
                pl.BlockSpec((1, rows, D), lambda i, p: (i, 0, 0)),
            ]
            + [pl.BlockSpec((D // 4, D), lambda i, p: (0, i))] * 4,
            out_specs=[
                resident((rows // 2, D)),
                resident((rows // 4, D)),
                resident((rows // 4, D)),
                resident((LANES, D)),
            ],
            scratch_shapes=[
                pltpu.VMEM((rows, D), F32),
                pltpu.VMEM((D, D), BF),
            ],
        ),
        out_shape=[sds((rows // 2, D), BF), *[sds((rows // 4, D), BF)] * 2, sds((LANES, D), F32)],
        cost_estimate=cost(6 * rows * D * D, 16 * rows * D + 6 * D * D, rows),
        compiler_params=pltpu.CompilerParams(vmem_limit_bytes=62 * MIB),
        name="norm_backward",
    )(scalars, tokens, mid_grad, vectors, small, g_inb, grads, *blocks)


def turn_kernel(pos_ref, turned_ref, columns_ref, d_ref, keep1_ref, send1_ref, keep2_ref, send2_ref):
    i = pl.program_id(0)
    parity = pos_ref[1]
    weights = contract(turned_ref[...], d_ref[0], ((1,), (0,)))

    @pl.when(i < 2)
    def _():
        put_parities(weights, parity, keep1_ref, send1_ref, pl.multiple_of(i * D, D))

    @pl.when(i == 2)
    def _():
        put_parities(weights, parity, keep2_ref, send2_ref, 0)
        put_parities(columns_ref[...].T, parity, keep2_ref, send2_ref, D)


def projection_grads(scalars, turned, columns, grads):
    rows = turned.shape[1]
    shards = lax.axis_size("shard")
    part1 = (shards // 2, D // shards, 2 * D)
    part2 = (shards // 2, D // shards, D + LANES)
    return pl.pallas_call(
        turn_kernel,
        grid_spec=pltpu.PrefetchScalarGridSpec(
            num_scalar_prefetch=1,
            grid=(3,),
            in_specs=[
                resident((D, rows)),
                resident((LANES, D)),
                pl.BlockSpec((1, rows, D), lambda i, p: (i, 0, 0)),
            ],
            out_specs=[resident(part1), resident(part1), resident(part2), resident(part2)],
        ),
        out_shape=[sds(part1, BF), sds(part1, BF), sds(part2, BF), sds(part2, BF)],
        cost_estimate=cost(6 * rows * D * D, 8 * rows * D + 6 * D * D, 0),
        compiler_params=pltpu.CompilerParams(vmem_limit_bytes=62 * MIB),
        name="projection_weight_grads",
    )(scalars, turned, columns, grads)


def by_shard(vector):
    shards = lax.axis_size("shard")
    count = vector.shape[1] // D
    return vector.reshape(shards, count, D // shards).transpose(1, 0, 2).reshape(count, D)


def layer(shards, vec, halves, ids, out_halves):
    qkv_shard, out_shard, in_shard, back_shard = shards
    me = lax.axis_index("seq").astype(jnp.int32)
    count = lax.axis_size("shard")
    mine = lax.axis_index("shard").astype(jnp.int32)
    near, far_axis = bits("seq")[0], bits("rep")
    direct = count == 4
    position = mine if direct else jnp.int32(0)
    scalars = jnp.stack([position, mine % 2, me])
    gather = lambda w: lax.all_gather(w, "shard", axis=0, tiled=True)
    to_core = lambda w: xor_send(w, "shard", 1)

    got_tokens = xor_send(pick(halves, 1 - me), "seq", 1)
    if direct:
        split = part_axes(back_shard)
        vec = vec.reshape(1, -1)
        across, vec_across = xor_send(qkv_shard, "shard", 2), xor_send(vec, "shard", 2)
        beside, vec_beside = to_core(qkv_shard), to_core(vec)
        across, vec_across, got_tokens, out_shard, in_shard, back_shard = tie(
            across, vec_across, got_tokens, out_shard, in_shard, back_shard
        )
        w_qkv = [qkv_shard, beside, across, to_core(across)]
        back_piece = fetch_part(back_shard, split)
        out_across = xor_send(out_shard, "shard", 2)
        out_beside, back_beside = to_core(out_shard), to_core(back_shard)
        near_two = jnp.concatenate([vec, vec_beside]).astype(F32)
        far_two = jnp.concatenate([vec_across, to_core(vec_across)]).astype(F32)
        odd, high = position % 2 == 1, position >= 2
        near_two = jnp.where(odd, near_two[::-1], near_two)
        far_two = jnp.where(odd, far_two[::-1], far_two)
        vec_all = jnp.where(
            high, jnp.concatenate([far_two, near_two]), jnp.concatenate([near_two, far_two])
        )
    else:
        w_qkv = quarters(gather(qkv_shard))
        vec_all = lax.all_gather(vec, "shard", axis=0).astype(F32)
    cell = D // count
    vectors = vec_all[:, : 8 * cell].reshape(count, 8, cell).transpose(1, 0, 2).reshape(8, D)
    in_bias = vec_all[:, 8 * cell :].reshape(1, -1)
    qkv, turned, tokens = first(scalars, halves, got_tokens, vectors, w_qkv)
    qkv, in_shard = tie(qkv, in_shard)
    w_in = gather(in_shard)
    same = ids[:, None] == jnp.arange(LANES, dtype=ids.dtype)[None, :]
    hot = same.astype(BF)
    far = jnp.where(same, 0.0, FAR).astype(BF)
    if direct:
        qkv, back_piece = tie(qkv, back_piece)
    for step in reversed(split[1:] if direct else []):
        back_piece = join(back_piece, step, 0)
    attn = attn_fwd(qkv, hot, far, 0, PAIRS // 2)
    *attn, out_halves = tie(*attn, out_halves)
    got_grad = xor_send(pick(out_halves, 1 - me), "seq", 1)
    if direct:
        *attn, back_piece, out_across = tie(*attn, back_piece, out_across)
        back_piece = join(back_piece, split[0], 0)
        w_out = [out_shard, out_beside, out_across, to_core(out_across)]
    attn, lse = attn_fwd(qkv, hot, far, PAIRS // 2, PAIRS - PAIRS // 2, attn)
    attn, got_grad, w_in = tie(attn, got_grad, w_in)
    if direct:
        attn, back_piece, w_out[3] = tie(attn, back_piece, w_out[3])
        w_back = [back_shard, back_beside, back_piece, to_core(back_piece)]
    else:
        w_out = quarters(gather(out_shard))
        w_back = quarters(gather(back_shard))
    own_out, other_out, mid_grad, attn_grad, keep, send, g_wback, g_inb, small = middle(
        scalars, tokens, attn, out_halves, got_grad, w_out, vectors, w_in, in_bias, w_back
    )
    s = lax.psum_scatter(g_wback, "shard", scatter_dimension=0, tiled=True)[None]
    got = to_core(send)
    got_out = xor_send(other_out, "seq", 1)
    grads = attn_bwd(qkv, attn_grad, hot, far, lse, 0, SPLIT)
    grads, got = tie(grads, got)
    first_far, rest_far = far_axis[0], far_axis[1:]
    by_axis = lambda v: v.reshape(v.shape[0], 2, 2, v.shape[1] // 4, v.shape[2])
    f = [by_axis(v) for v in (keep, got)]
    wide = f[0].shape[4]
    middle_col = LANES * (wide // (2 * LANES))
    f1 = halve([v[..., :middle_col] for v in f], near, 1)
    f2 = halve([v[..., middle_col:] for v in f], first_far, 2)
    grads = attn_bwd(qkv, attn_grad, hot, far, lse, SPLIT, PAIRS - SPLIT, [grads])
    grads, got_out, s, f1, f2 = tie(grads, got_out, s, f1, f2)
    f1, f2 = halve(f1, first_far, 2), halve(f2, near, 1)
    s = halve((s, jnp.zeros_like(s)), near, 1)
    own_grad, other1, other2, columns = last(
        scalars, tokens, mid_grad, vectors, small, by_shard(g_inb), grads, w_qkv
    )
    columns, other1, other2, f1, f2, s = tie(columns, other1, other2, f1, f2, s)
    f = chips([jnp.concatenate([v, w], axis=4) for v, w in zip(f1, f2)])
    s = halve(s, first_far, 1)
    got1, got2 = xor_send(other1, "seq", 1), xor_send(other2, "seq", 1)
    a_keep, a_send, b_keep, b_send = projection_grads(scalars, turned, columns, grads)

    a_send, b_send, f, s, got1 = tie(a_send, b_send, f, s, got1)
    a, b = (a_keep, to_core(a_send)), (b_keep, to_core(b_send))
    a, b, f = tie(a, b, f)
    a, b = chips(a), halve(b, near, 1)
    f = last_steps(f, rest_far)
    a, b, f, got2 = tie(a, b, f, got2)
    a, b = halve(a, near, 1), chips(b)
    s = last_steps(s, rest_far)
    f = join(f, first_far, 2)
    a, b, f = tie(a, b, f)
    t = halve([jnp.concatenate([v, w], axis=2) for v, w in zip(a, b)], first_far, 1)
    f = join(f, near, 1)
    t, s = tie(t, s)
    t = last_steps(t, rest_far)
    s = join(s, first_far, 1)
    t, f, s = tie(t, f, s)
    t = join(t, first_far, 1)
    s = join(s, near, 1)
    t, s = tie(t, s)
    t = join(t, near, 1)
    f, got1, got2 = tie(f, got1, got2)
    got_grad = jnp.concatenate([got1, got2], axis=0)
    outputs = [
        jnp.stack([jnp.where(me == 0, kept, got), jnp.where(me == 0, got, kept)])
        for kept, got in ((own_out, got_out), (own_grad, got_grad))
    ]
    flat = lambda v: v[0].reshape(-1, v.shape[-1]).astype(F32)
    return outputs[0], outputs[1], [s[0].astype(F32), flat(f), flat(t)]


def last_steps(state, order):
    for step in order:
        state = whole(state, step)
    return added(state)


def body(
    tokens,
    segment_ids,
    out_grad,
    norm1_gain,
    norm1_bias,
    qkv_weight,
    query_bias,
    value_bias,
    out_weight,
    out_bias,
    norm2_gain,
    norm2_bias,
    ff_in_weight,
    ff_in_bias,
    ff_out_weight,
    ff_out_bias,
):
    seqs, row_count, _ = tokens.shape
    ways = lax.axis_size("seq")
    me = lax.axis_index("seq")
    wide = ff_in_weight.shape[1]

    vec = jnp.concatenate(
        [
            norm1_gain,
            norm1_bias,
            query_bias,
            value_bias,
            out_bias,
            norm2_gain,
            norm2_bias,
            ff_out_bias,
            ff_in_bias,
        ]
    )
    weights = (qkv_weight, out_weight, ff_in_weight, ff_out_weight)

    out_parts, grad_parts, sums = [], [], None
    for lo in range(0, seqs, ways):
        ids = pick(segment_ids[lo : lo + ways], me)
        block, tgrad, terms = layer(
            weights, vec, tokens[lo : lo + ways], ids, out_grad[lo : lo + ways]
        )
        out_parts.append(block)
        grad_parts.append(tgrad)
        sums = terms if sums is None else [a + b for a, b in zip(sums, terms)]
    g_wback, g_in, g_t = sums
    small = g_t[:, 3 * D : 3 * D + 8 + g_in.shape[1] // D - 1].T
    return (
        jnp.concatenate(out_parts, axis=0),
        jnp.concatenate(grad_parts, axis=0),
        small[0],
        small[1],
        g_t[:, : 3 * D],
        small[2],
        small[3],
        g_in[:, wide:],
        small[4],
        small[5],
        small[6],
        g_in[:, :wide],
        small[8:].reshape(-1),
        g_wback,
        small[7],
    )


def solution(mesh):
    in_specs = (
        P(("shard", "rep"), "seq", None),
        P(("shard", "rep"), None),
        P(("shard", "rep"), "seq", None),
        P("shard"),
        P("shard"),
        P("shard", None),
        P("shard"),
        P("shard"),
        P("shard", None),
        P("shard"),
        P("shard"),
        P("shard"),
        P("shard", None),
        P("shard"),
        P("shard", None),
        P("shard"),
    )
    out_specs = (
        P(("shard", "rep"), "seq", None),
        P(("shard", "rep"), "seq", None),
        P("shard"),
        P("shard"),
        P("shard", None),
        P("shard"),
        P("shard"),
        P("shard", None),
        P("shard"),
        P("shard"),
        P("shard"),
        P("shard", None),
        P("shard"),
        P("shard", None),
        P("shard"),
    )
    return jax.shard_map(body, mesh=mesh, in_specs=in_specs, out_specs=out_specs, check_vma=False)
```

```python
import jax
import jax.numpy as jnp
from jax import lax
from jax.experimental import pallas as pl
from jax.experimental.pallas import tpu as pltpu
from jax.sharding import PartitionSpec as P

D = 768
HEADS = 12
HEAD_DIM = 64
LANES = 128
HB = 512
SPLIT = 2
PAIRS = HEADS // 2
FAR = -1e30
BF = jnp.bfloat16
F32 = jnp.float32
MIB = 1 << 20


def xor_send(value, axis, mask):
    size = lax.axis_size(axis)
    return lax.ppermute(value, axis, [(i, i ^ mask) for i in range(size)])


def bits(axis):
    return [(axis, 1 << b) for b in range((lax.axis_size(axis) - 1).bit_length())]


def bit_of(axis, mask):
    return (lax.axis_index(axis) // mask) % 2


def pick(stacked, index):
    return lax.dynamic_index_in_dim(stacked, index, 0, keepdims=False)


def tie(*values):
    return lax.optimization_barrier(values)


def added(state):
    return (state[0].astype(F32) + state[1].astype(F32)).astype(state[0].dtype)


def cut_half(state, step, dim):
    bit = bit_of(*step)
    size = state[0].shape[dim] // 2
    cut = lambda at: added([lax.dynamic_slice_in_dim(s, at * size, size, dim) for s in state])
    return cut(bit), cut(1 - bit)


def send_half(parts, step):
    return parts[0], xor_send(parts[1], *step)


def halve(state, step, dim):
    return send_half(cut_half(state, step, dim), step)


def whole(state, step):
    value = added(state)
    return value, xor_send(value, *step)


def join(part, step, dim):
    bit = bit_of(*step)
    other = xor_send(part, *step)
    low = jnp.where(bit == 0, part, other)
    high = jnp.where(bit == 0, other, part)
    return jnp.concatenate([low, high], axis=dim)


def cut_chips(state, mask):
    bit = bit_of("shard", mask)

    def cut(at):
        split = [s.reshape((s.shape[0] // 2, 2) + s.shape[1:]) for s in state]
        return added([lax.dynamic_index_in_dim(s, at, 1, keepdims=False) for s in split])

    return cut(bit), cut(1 - bit)


def chips(state, mask=2):
    while mask < lax.axis_size("shard"):
        state = send_half(cut_chips(state, mask), ("shard", mask))
        mask *= 2
    return state


def quarters(full):
    rows = full.shape[0] // 4
    return [full[k * rows : (k + 1) * rows] for k in range(4)]


def part_axes(shard):
    parts = bits("rep")[:1] + bits("seq")
    return parts if shard.shape[0] % (8 << len(parts)) == 0 else []


def fetch_part(shard, parts):
    piece = shard
    for axis, mask in parts:
        half = piece.shape[0] // 2
        piece = lax.dynamic_slice_in_dim(piece, bit_of(axis, mask) * half, half)
    return xor_send(piece, "shard", 2)


def cost(flops, bytes_accessed, transcendentals):
    return pl.CostEstimate(
        flops=flops, bytes_accessed=bytes_accessed, transcendentals=transcendentals
    )


def sds(shape, dtype):
    return jax.ShapeDtypeStruct(shape, dtype)


def fixed(shape):
    return pl.BlockSpec(shape, lambda i: (0,) * len(shape), pipeline_mode=pl.Buffered(1))


def contract(left, right, dims):
    return lax.dot_general(left, right, (dims, ((), ())), preferred_element_type=F32)


def row_stats(rows):
    mean = jnp.mean(rows, axis=-1, keepdims=True)
    centered = rows - mean
    rstd = lax.rsqrt(jnp.mean(centered * centered, axis=-1, keepdims=True) + 1e-06)
    return centered * rstd, rstd


def norm_back(in_grad, normal, rstd, gain):
    scaled = in_grad * gain
    mean_e = jnp.mean(scaled, axis=-1, keepdims=True)
    mean_en = jnp.mean(scaled * normal, axis=-1, keepdims=True)
    return rstd * (scaled - mean_e - normal * mean_en)


def put_parities(value, parity, keep_ref, send_ref, at):
    blocks, rows = keep_ref.shape[0], keep_ref.shape[1]
    cols = pl.ds(at, value.shape[1])
    for k in range(blocks):
        even = value[2 * k * rows : (2 * k + 1) * rows]
        odd = value[(2 * k + 1) * rows : (2 * k + 2) * rows]
        keep_ref[k, :, cols] = jnp.where(parity == 0, even, odd).astype(keep_ref.dtype)
        send_ref[k, :, cols] = jnp.where(parity == 0, odd, even).astype(send_ref.dtype)


def place(ref, blocks, position):
    rows = blocks[0].shape[0]
    for k, block in enumerate(blocks):
        at = pl.multiple_of((position ^ k) * rows, rows)
        ref[pl.ds(at, rows), :] = block[...]


def first_kernel(pos_ref, kept_ref, got_ref, vec_ref, w0, w1, w2, w3, qkv_ref, turned_ref, tok_ref, normed_ref, w_ref):
    i = pl.program_id(0)

    @pl.when(i == 0)
    def _():
        place(tok_ref, (kept_ref.at[0], got_ref), pos_ref[2])
        n, _ = row_stats(tok_ref[...].astype(F32))
        x = (n * vec_ref[0:1, :] + vec_ref[1:2, :]).astype(BF)
        normed_ref[...] = x
        turned_ref[...] = x.T

    place(w_ref, (w0, w1, w2, w3), pos_ref[0])
    bias = jnp.where(i == 0, vec_ref[2:3, :], jnp.where(i == 2, vec_ref[3:4, :], 0.0))
    qkv_ref[...] = (contract(normed_ref[...], w_ref[...], ((1,), (0,))) + bias).astype(BF)


def resident(shape):
    return pl.BlockSpec(shape, lambda i, p: (0,) * len(shape), pipeline_mode=pl.Buffered(1))


def kept_half(rows):
    return pl.BlockSpec((1, rows, D), lambda i, p: (p[2], 0, 0), pipeline_mode=pl.Buffered(1))


def first(scalars, halves, got, vectors, blocks):
    half = halves.shape[1]
    rows = 2 * half
    across = lambda height: pl.BlockSpec((height, D), lambda i, p: (0, i))
    return pl.pallas_call(
        first_kernel,
        grid_spec=pltpu.PrefetchScalarGridSpec(
            num_scalar_prefetch=1,
            grid=(3,),
            in_specs=[kept_half(half), resident((half, D)), resident(vectors.shape)]
            + [across(D // 4)] * 4,
            out_specs=[across(rows), resident((D, rows)), resident((rows, D))],
            scratch_shapes=[pltpu.VMEM((rows, D), BF), pltpu.VMEM((D, D), BF)],
        ),
        out_shape=[sds((rows, 3 * D), BF), sds((D, rows), BF), sds((rows, D), BF)],
        cost_estimate=cost(6 * rows * D * D, 12 * rows * D + 6 * D * D, rows),
        compiler_params=pltpu.CompilerParams(vmem_limit_bytes=62 * MIB),
        name="norm_and_projections",
    )(scalars, halves, got, vectors, *blocks)


def by_head(rows):
    lane = lax.broadcasted_iota(jnp.int32, rows.shape, 1)
    zero = jnp.zeros_like(rows)
    return jnp.concatenate(
        [jnp.where(lane < HEAD_DIM, rows, zero), jnp.where(lane >= HEAD_DIM, rows, zero)], axis=0
    )


def own_rows(both, width):
    return jnp.concatenate([both[:HEAD_DIM, :width], both[HEAD_DIM:, width:]], axis=0)


def query_side(q_ref, hot_ref):
    hot = hot_ref[...]
    q = by_head(q_ref[...] * jnp.asarray(HEAD_DIM**-0.5, BF))
    return jnp.concatenate([q, jnp.concatenate([hot, hot], axis=0)], axis=1)


def attn_fwd_kernel(q_ref, k_ref, v_ref, hot_ref, far_ref, *rest):
    o_ref, lse_ref = rest[-2:]
    width = q_ref.shape[0]
    qs = query_side(q_ref, hot_ref)
    ks = jnp.concatenate([k_ref[...], far_ref[...]], axis=1)
    s = contract(ks, qs, ((1,), (1,)))
    top = jnp.max(s, axis=0, keepdims=True)
    e = jnp.exp(s - top)
    tot = jnp.sum(e, axis=0, keepdims=True)
    o = contract(v_ref[...], e.astype(BF), ((0,), (0,))) * (1.0 / tot)
    o_ref[...] = own_rows(o, width).T.astype(BF)
    lse_ref[0] = top + jnp.log(tot)


def pair_cols(rows, at):
    return pl.BlockSpec((rows, LANES), lambda p: (0, at + p))


def attn_fwd(qkv, hot, far, at, count, before=()):
    rows = qkv.shape[0]
    return pl.pallas_call(
        attn_fwd_kernel,
        grid=(count,),
        in_specs=[
            pair_cols(rows, at),
            pair_cols(rows, PAIRS + at),
            pair_cols(rows, 2 * PAIRS + at),
            fixed((rows, LANES)),
            fixed((rows, LANES)),
        ]
        + [pl.BlockSpec(memory_space=pl.ANY)] * len(before),
        out_specs=[pair_cols(rows, at), pl.BlockSpec((1, 1, 2 * rows), lambda p: (at + p, 0, 0))],
        out_shape=[sds((rows, D), BF), sds((PAIRS, 1, 2 * rows), F32)],
        input_output_aliases={5 + i: i for i in range(len(before))},
        cost_estimate=cost(
            16 * rows * rows * LANES * count, 8 * rows * LANES * count, 2 * count * rows * rows
        ),
        compiler_params=pltpu.CompilerParams(vmem_limit_bytes=62 * MIB),
        name="attention_forward",
    )(qkv, qkv, qkv, hot, far, *before)


def attn_bwd_kernel(
    q_ref, k_ref, v_ref, do_ref, hot_ref, far_ref, lse_ref, *rest
):
    grad_ref = rest[-1]
    width = q_ref.shape[0]
    qs = query_side(q_ref, hot_ref)
    do = by_head(do_ref[...])
    keys = k_ref[...]
    ks = jnp.concatenate([keys, far_ref[...]], axis=1)
    s = contract(ks, qs, ((1,), (1,)))
    p = jnp.exp(s - lse_ref[0])
    dp = contract(v_ref[...], do, ((1,), (1,)))
    t = p * dp
    inner = jnp.sum(t, axis=0, keepdims=True)
    ds = (t - p * inner).astype(BF)
    grad_ref[2] = contract(p.astype(BF), do, ((1,), (0,))).astype(BF)
    grad_ref[1] = contract(ds, qs[:, :LANES], ((1,), (0,))).astype(BF)
    dq = own_rows(contract(keys, ds, ((0,), (0,))), width)
    grad_ref[0] = (dq * HEAD_DIM**-0.5).T.astype(BF)


def attn_bwd(qkv, dout, hot, far, lse, at, count, before=()):
    rows = qkv.shape[0]
    return pl.pallas_call(
        attn_bwd_kernel,
        grid=(count,),
        in_specs=[
            pair_cols(rows, at),
            pair_cols(rows, PAIRS + at),
            pair_cols(rows, 2 * PAIRS + at),
            pair_cols(rows, at),
            fixed((rows, LANES)),
            fixed((rows, LANES)),
            pl.BlockSpec((1, 1, 2 * rows), lambda p: (at + p, 0, 0)),
        ]
        + [pl.BlockSpec(memory_space=pl.ANY)] * len(before),
        out_specs=pl.BlockSpec((3, rows, LANES), lambda p: (0, 0, at + p)),
        out_shape=sds((3, rows, D), BF),
        input_output_aliases={7 + i: i for i in range(len(before))},
        cost_estimate=cost(
            10 * rows * rows * LANES * count * 4, 14 * rows * LANES * count, 2 * count * rows * rows
        ),
        compiler_params=pltpu.CompilerParams(vmem_limit_bytes=62 * MIB),
        name="attention_backward",
    )(qkv, qkv, qkv, dout, hot, far, lse, *before)


def put_halves(rows, mine, own_ref, other_ref):
    half = own_ref.shape[0]
    low, high = rows[:half], rows[half:]
    own_ref[...] = jnp.where(mine == 0, low, high)
    other_ref[...] = jnp.where(mine == 0, high, low)


def middle_kernel(
    par_ref, tok_ref, attn_ref, gkept_ref, ggot_ref, wo0, wo1, wo2, wo3, vec_ref, wi_ref, ib_ref, wb0, wb1, wb2, wb3,
    own_ref, other_ref, mid_ref, agrad_ref, keep_ref, send_ref, gwb_ref, gib_ref, small_ref,
    resid, normed, normed_t, out_acc, in_acc, g_ref, wo_ref, wb_all, arrived,
):
    i = pl.program_id(0)
    parity = par_ref[1]

    def fetch(k, block):
        rows = block.shape[0]
        at = pl.multiple_of((par_ref[0] ^ k) * rows, rows)
        return pltpu.make_async_copy(block, wb_all.at[pl.ds(at, rows)], arrived.at[k])

    @pl.when(i == 0)
    def _():
        for k, block in enumerate((wb0, wb1, wb2, wb3)):
            fetch(k, block).start()
        place(g_ref, (gkept_ref.at[0], ggot_ref), par_ref[2])
        place(wo_ref, (wo0, wo1, wo2, wo3), par_ref[0])
        r = tok_ref[...].astype(F32) + contract(attn_ref[...], wo_ref[...], ((1,), (0,))) + vec_ref[4:5, :]
        resid[...] = r
        n, _ = row_stats(r)
        x = (n * vec_ref[5:6, :] + vec_ref[6:7, :]).astype(BF)
        normed[...] = x
        normed_t[...] = x.T
        out_acc[...] = jnp.zeros_like(out_acc)
        in_acc[...] = jnp.zeros_like(in_acc)
        for k, block in enumerate((wb0, wb1, wb2, wb3)):
            fetch(k, block).wait()

    x = normed[...]
    g = g_ref[...]
    wi = wi_ref[...]
    wb = wb_all[pl.ds(pl.multiple_of(i * HB, HB), HB), :]
    pre = contract(x, wi, ((1,), (0,))) + ib_ref[...]
    cdf = 0.5 + 0.5 * lax.erf(pre * 0.7071067811865476)
    h = (pre * cdf).astype(BF)
    slope = cdf + pre * (0.3989422804014327 * jnp.exp(-0.5 * (pre * pre)))
    pg = (contract(g, wb, ((1,), (1,))) * slope).astype(BF)
    out_acc[...] += contract(h, wb, ((1,), (0,)))
    in_acc[...] += contract(pg, wi, ((1,), (1,)))
    at = pl.multiple_of(i * HB, HB)
    put_parities(contract(normed_t[...], pg, ((1,), (0,))), parity, keep_ref, send_ref, at)
    gwb_ref[...] = contract(h, g, ((0,), (0,))).astype(BF)
    gib_ref[...] = jnp.sum(pg.astype(F32), axis=0, keepdims=True)

    @pl.when(i == pl.num_programs(0) - 1)
    def _():
        r = resid[...]
        put_halves((r + out_acc[...] + vec_ref[7:8, :]).astype(BF), par_ref[2], own_ref, other_ref)
        n, rstd = row_stats(r)
        d = in_acc[...]
        gf = g_ref[...].astype(F32)
        m = gf + norm_back(d, n, rstd, vec_ref[5:6, :])
        mid_ref[...] = m
        b = m.astype(BF)
        small_ref[0:1, :] = jnp.sum(b.astype(F32), axis=0, keepdims=True)
        small_ref[1:2, :] = jnp.sum(d * n, axis=0, keepdims=True)
        small_ref[2:3, :] = jnp.sum(d, axis=0, keepdims=True)
        small_ref[3:4, :] = jnp.sum(gf, axis=0, keepdims=True)
        agrad_ref[...] = contract(b, wo_ref[...], ((1,), (1,))).astype(BF)
        put_parities(
            contract(attn_ref[...], b, ((0,), (0,))), parity, keep_ref, send_ref,
            keep_ref.shape[2] - D,
        )


def middle(scalars, tokens, attn, halves, got, w_out, vectors, w_in, in_bias, w_back):
    rows = tokens.shape[0]
    ff = w_in.shape[1]
    shards = lax.axis_size("shard")
    half = (shards // 2, D // shards, ff + D)
    return pl.pallas_call(
        middle_kernel,
        grid_spec=pltpu.PrefetchScalarGridSpec(
            num_scalar_prefetch=1,
            grid=(ff // HB,),
            in_specs=[
                resident((rows, D)),
                resident((rows, D)),
                kept_half(rows // 2),
                resident((rows // 2, D)),
            ]
            + [resident((D // 4, D))] * 4
            + [resident(vectors.shape)]
            + [
                pl.BlockSpec((D, HB), lambda i, p: (0, i)),
                pl.BlockSpec((1, HB), lambda i, p: (0, i)),
            ]
            + [pl.BlockSpec(memory_space=pl.ANY)] * 4,
            out_specs=[
                resident((rows // 2, D)),
                resident((rows // 2, D)),
                resident((rows, D)),
                resident((rows, D)),
                resident(half),
                resident(half),
                pl.BlockSpec((HB, D), lambda i, p: (i, 0)),
                pl.BlockSpec((1, HB), lambda i, p: (0, i)),
                resident((8, D)),
            ],
            scratch_shapes=[
                pltpu.VMEM((rows, D), F32),
                pltpu.VMEM((rows, D), BF),
                pltpu.VMEM((D, rows), BF),
                pltpu.VMEM((rows, D), F32),
                pltpu.VMEM((rows, D), F32),
                pltpu.VMEM((rows, D), BF),
                pltpu.VMEM((D, D), BF),
                pltpu.VMEM((ff, D), BF),
                pltpu.SemaphoreType.DMA((4,)),
            ],
        ),
        out_shape=[
            sds((rows // 2, D), BF),
            sds((rows // 2, D), BF),
            sds((rows, D), F32),
            sds((rows, D), BF),
            sds(half, BF),
            sds(half, BF),
            sds((ff, D), BF),
            sds((1, ff), F32),
            sds((8, D), F32),
        ],
        cost_estimate=cost(2 * rows * D * (6 * ff + 3 * D), 10 * D * ff + 20 * rows * D, 2 * rows * ff),
        compiler_params=pltpu.CompilerParams(vmem_limit_bytes=62 * MIB),
        name="projection_and_feed_forward",
    )(scalars, tokens, attn, halves, got, *w_out, vectors, w_in, in_bias, *w_back)


def last_kernel(
    pos_ref, tok_ref, mid_ref, vec_ref, small_ref, gib_ref, d_ref, w0, w1, w2, w3,
    own_ref, other1_ref, other2_ref, columns, total, w_ref,
):
    i = pl.program_id(0)
    d = d_ref[0]

    @pl.when(i == 0)
    def _():
        columns[...] = jnp.zeros_like(columns)
        columns[4:8, :] = small_ref[0:4, :]
        columns[8 : 8 + gib_ref.shape[0], :] = gib_ref[...]
        total[...] = jnp.zeros_like(total)
        columns[2:3, :] = jnp.sum(d.astype(F32), axis=0, keepdims=True)

    place(w_ref, (w0, w1, w2, w3), pos_ref[0])
    total[...] += contract(d, w_ref[...], ((1,), (1,)))

    @pl.when(i == 2)
    def _():
        columns[3:4, :] = jnp.sum(d.astype(F32), axis=0, keepdims=True)
        t = total[...]
        n, rstd = row_stats(tok_ref[...].astype(F32))
        token_grad = (mid_ref[...] + norm_back(t, n, rstd, vec_ref[0:1, :])).astype(BF)
        half = own_ref.shape[0]
        low, high = token_grad[:half], token_grad[half:]
        own_ref[...] = jnp.where(pos_ref[2] == 0, low, high)
        other = jnp.where(pos_ref[2] == 0, high, low)
        other1_ref[...] = other[: half // 2]
        other2_ref[...] = other[half // 2 :]
        columns[0:1, :] = jnp.sum(t * n, axis=0, keepdims=True)
        columns[1:2, :] = jnp.sum(t, axis=0, keepdims=True)


def last(scalars, tokens, mid_grad, vectors, small, g_inb, grads, blocks):
    rows = tokens.shape[0]
    return pl.pallas_call(
        last_kernel,
        grid_spec=pltpu.PrefetchScalarGridSpec(
            num_scalar_prefetch=1,
            grid=(3,),
            in_specs=[
                resident((rows, D)),
                resident((rows, D)),
                resident(vectors.shape),
                resident((8, D)),
                resident(g_inb.shape),
                pl.BlockSpec((1, rows, D), lambda i, p: (i, 0, 0)),
            ]
            + [pl.BlockSpec((D // 4, D), lambda i, p: (0, i))] * 4,
            out_specs=[
                resident((rows // 2, D)),
                resident((rows // 4, D)),
                resident((rows // 4, D)),
                resident((LANES, D)),
            ],
            scratch_shapes=[
                pltpu.VMEM((rows, D), F32),
                pltpu.VMEM((D, D), BF),
            ],
        ),
        out_shape=[sds((rows // 2, D), BF), *[sds((rows // 4, D), BF)] * 2, sds((LANES, D), F32)],
        cost_estimate=cost(6 * rows * D * D, 16 * rows * D + 6 * D * D, rows),
        compiler_params=pltpu.CompilerParams(vmem_limit_bytes=62 * MIB),
        name="norm_backward",
    )(scalars, tokens, mid_grad, vectors, small, g_inb, grads, *blocks)


def turn_kernel(pos_ref, turned_ref, columns_ref, d_ref, keep1_ref, send1_ref, keep2_ref, send2_ref):
    i = pl.program_id(0)
    parity = pos_ref[1]
    weights = contract(turned_ref[...], d_ref[0], ((1,), (0,)))

    @pl.when(i < 2)
    def _():
        put_parities(weights, parity, keep1_ref, send1_ref, pl.multiple_of(i * D, D))

    @pl.when(i == 2)
    def _():
        put_parities(weights, parity, keep2_ref, send2_ref, 0)
        put_parities(columns_ref[...].T, parity, keep2_ref, send2_ref, D)


def projection_grads(scalars, turned, columns, grads):
    rows = turned.shape[1]
    shards = lax.axis_size("shard")
    part1 = (shards // 2, D // shards, 2 * D)
    part2 = (shards // 2, D // shards, D + LANES)
    return pl.pallas_call(
        turn_kernel,
        grid_spec=pltpu.PrefetchScalarGridSpec(
            num_scalar_prefetch=1,
            grid=(3,),
            in_specs=[
                resident((D, rows)),
                resident((LANES, D)),
                pl.BlockSpec((1, rows, D), lambda i, p: (i, 0, 0)),
            ],
            out_specs=[resident(part1), resident(part1), resident(part2), resident(part2)],
        ),
        out_shape=[sds(part1, BF), sds(part1, BF), sds(part2, BF), sds(part2, BF)],
        cost_estimate=cost(6 * rows * D * D, 8 * rows * D + 6 * D * D, 0),
        compiler_params=pltpu.CompilerParams(vmem_limit_bytes=62 * MIB),
        name="projection_weight_grads",
    )(scalars, turned, columns, grads)


def by_shard(vector):
    shards = lax.axis_size("shard")
    count = vector.shape[1] // D
    return vector.reshape(shards, count, D // shards).transpose(1, 0, 2).reshape(count, D)


def layer(shards, vec, halves, ids, out_halves):
    qkv_shard, out_shard, in_shard, back_shard = shards
    me = lax.axis_index("seq").astype(jnp.int32)
    count = lax.axis_size("shard")
    mine = lax.axis_index("shard").astype(jnp.int32)
    near, far_axis = bits("seq")[0], bits("rep")
    direct = count == 4
    position = mine if direct else jnp.int32(0)
    scalars = jnp.stack([position, mine % 2, me])
    gather = lambda w: lax.all_gather(w, "shard", axis=0, tiled=True)
    to_core = lambda w: xor_send(w, "shard", 1)

    got_tokens = xor_send(pick(halves, 1 - me), "seq", 1)
    if direct:
        split = part_axes(back_shard)
        vec = vec.reshape(1, -1)
        across, vec_across = xor_send(qkv_shard, "shard", 2), xor_send(vec, "shard", 2)
        beside, vec_beside = to_core(qkv_shard), to_core(vec)
        across, vec_across, got_tokens, out_shard, in_shard, back_shard = tie(
            across, vec_across, got_tokens, out_shard, in_shard, back_shard
        )
        w_qkv = [qkv_shard, beside, across, to_core(across)]
        back_piece = fetch_part(back_shard, split)
        out_across = xor_send(out_shard, "shard", 2)
        out_beside, back_beside = to_core(out_shard), to_core(back_shard)
        near_two = jnp.concatenate([vec, vec_beside]).astype(F32)
        far_two = jnp.concatenate([vec_across, to_core(vec_across)]).astype(F32)
        odd, high = position % 2 == 1, position >= 2
        near_two = jnp.where(odd, near_two[::-1], near_two)
        far_two = jnp.where(odd, far_two[::-1], far_two)
        vec_all = jnp.where(
            high, jnp.concatenate([far_two, near_two]), jnp.concatenate([near_two, far_two])
        )
    else:
        w_qkv = quarters(gather(qkv_shard))
        vec_all = lax.all_gather(vec, "shard", axis=0).astype(F32)
    cell = D // count
    vectors = vec_all[:, : 8 * cell].reshape(count, 8, cell).transpose(1, 0, 2).reshape(8, D)
    in_bias = vec_all[:, 8 * cell :].reshape(1, -1)
    qkv, turned, tokens = first(scalars, halves, got_tokens, vectors, w_qkv)
    w_in = gather(in_shard)
    same = ids[:, None] == jnp.arange(LANES, dtype=ids.dtype)[None, :]
    hot = same.astype(BF)
    far = jnp.where(same, 0.0, FAR).astype(BF)
    if direct:
        qkv, back_piece = tie(qkv, back_piece)
    for step in reversed(split[1:] if direct else []):
        back_piece = join(back_piece, step, 0)
    attn = attn_fwd(qkv, hot, far, 0, PAIRS // 3)
    *attn, out_halves = tie(*attn, out_halves)
    got_grad = xor_send(pick(out_halves, 1 - me), "seq", 1)
    if direct:
        *attn, back_piece, out_across = tie(*attn, back_piece, out_across)
        back_piece = join(back_piece, split[0], 0)
        w_out = [out_shard, out_beside, out_across, to_core(out_across)]
    attn, lse = attn_fwd(qkv, hot, far, PAIRS // 3, PAIRS - PAIRS // 3, attn)
    attn, got_grad, w_in = tie(attn, got_grad, w_in)
    if direct:
        attn, back_piece, w_out[3] = tie(attn, back_piece, w_out[3])
        w_back = [back_shard, back_beside, back_piece, to_core(back_piece)]
    else:
        w_out = quarters(gather(out_shard))
        w_back = quarters(gather(back_shard))
    own_out, other_out, mid_grad, attn_grad, keep, send, g_wback, g_inb, small = middle(
        scalars, tokens, attn, out_halves, got_grad, w_out, vectors, w_in, in_bias, w_back
    )
    s = lax.psum_scatter(g_wback, "shard", scatter_dimension=0, tiled=True)[None]
    got = to_core(send)
    got_out = xor_send(other_out, "seq", 1)
    grads = attn_bwd(qkv, attn_grad, hot, far, lse, 0, SPLIT)
    grads, got = tie(grads, got)
    first_far, rest_far = far_axis[0], far_axis[1:]
    by_axis = lambda v: v.reshape(v.shape[0], 2, 2, v.shape[1] // 4, v.shape[2])
    f = [by_axis(v) for v in (keep, got)]
    wide = f[0].shape[4]
    middle_col = LANES * (wide // (2 * LANES))
    f1 = halve([v[..., :middle_col] for v in f], near, 1)
    f2 = halve([v[..., middle_col:] for v in f], first_far, 2)
    grads = attn_bwd(qkv, attn_grad, hot, far, lse, SPLIT, PAIRS - SPLIT, [grads])
    grads, got_out, s, f1, f2 = tie(grads, got_out, s, f1, f2)
    f1, f2 = halve(f1, first_far, 2), halve(f2, near, 1)
    s = halve((s, jnp.zeros_like(s)), near, 1)
    own_grad, other1, other2, columns = last(
        scalars, tokens, mid_grad, vectors, small, by_shard(g_inb), grads, w_qkv
    )
    columns, other1, other2, f1, f2, s = tie(columns, other1, other2, f1, f2, s)
    f = chips([jnp.concatenate([v, w], axis=4) for v, w in zip(f1, f2)])
    s = halve(s, first_far, 1)
    got1, got2 = xor_send(other1, "seq", 1), xor_send(other2, "seq", 1)
    a_keep, a_send, b_keep, b_send = projection_grads(scalars, turned, columns, grads)

    a_send, b_send, f, s, got1 = tie(a_send, b_send, f, s, got1)
    a, b = (a_keep, to_core(a_send)), (b_keep, to_core(b_send))
    a, b, f = tie(a, b, f)
    a, b = chips(a), halve(b, near, 1)
    f = last_steps(f, rest_far)
    a, b, f, got2 = tie(a, b, f, got2)
    a, b = halve(a, near, 1), chips(b)
    s = last_steps(s, rest_far)
    f = join(f, first_far, 2)
    a, b, f = tie(a, b, f)
    t = halve([jnp.concatenate([v, w], axis=2) for v, w in zip(a, b)], first_far, 1)
    f = join(f, near, 1)
    t, s = tie(t, s)
    t = last_steps(t, rest_far)
    s = join(s, first_far, 1)
    t, f, s = tie(t, f, s)
    t = join(t, first_far, 1)
    s = join(s, near, 1)
    t, s = tie(t, s)
    t = join(t, near, 1)
    f, got1, got2 = tie(f, got1, got2)
    got_grad = jnp.concatenate([got1, got2], axis=0)
    outputs = [
        jnp.stack([jnp.where(me == 0, kept, got), jnp.where(me == 0, got, kept)])
        for kept, got in ((own_out, got_out), (own_grad, got_grad))
    ]
    flat = lambda v: v[0].reshape(-1, v.shape[-1]).astype(F32)
    return outputs[0], outputs[1], [s[0].astype(F32), flat(f), flat(t)]


def last_steps(state, order):
    for step in order:
        state = whole(state, step)
    return added(state)


def body(
    tokens,
    segment_ids,
    out_grad,
    norm1_gain,
    norm1_bias,
    qkv_weight,
    query_bias,
    value_bias,
    out_weight,
    out_bias,
    norm2_gain,
    norm2_bias,
    ff_in_weight,
    ff_in_bias,
    ff_out_weight,
    ff_out_bias,
):
    seqs, row_count, _ = tokens.shape
    ways = lax.axis_size("seq")
    me = lax.axis_index("seq")
    wide = ff_in_weight.shape[1]

    vec = jnp.concatenate(
        [
            norm1_gain,
            norm1_bias,
            query_bias,
            value_bias,
            out_bias,
            norm2_gain,
            norm2_bias,
            ff_out_bias,
            ff_in_bias,
        ]
    )
    weights = (qkv_weight, out_weight, ff_in_weight, ff_out_weight)

    out_parts, grad_parts, sums = [], [], None
    for lo in range(0, seqs, ways):
        ids = pick(segment_ids[lo : lo + ways], me)
        block, tgrad, terms = layer(
            weights, vec, tokens[lo : lo + ways], ids, out_grad[lo : lo + ways]
        )
        out_parts.append(block)
        grad_parts.append(tgrad)
        sums = terms if sums is None else [a + b for a, b in zip(sums, terms)]
    g_wback, g_in, g_t = sums
    small = g_t[:, 3 * D : 3 * D + 8 + g_in.shape[1] // D - 1].T
    return (
        jnp.concatenate(out_parts, axis=0),
        jnp.concatenate(grad_parts, axis=0),
        small[0],
        small[1],
        g_t[:, : 3 * D],
        small[2],
        small[3],
        g_in[:, wide:],
        small[4],
        small[5],
        small[6],
        g_in[:, :wide],
        small[8:].reshape(-1),
        g_wback,
        small[7],
    )


def solution(mesh):
    in_specs = (
        P(("shard", "rep"), "seq", None),
        P(("shard", "rep"), None),
        P(("shard", "rep"), "seq", None),
        P("shard"),
        P("shard"),
        P("shard", None),
        P("shard"),
        P("shard"),
        P("shard", None),
        P("shard"),
        P("shard"),
        P("shard"),
        P("shard", None),
        P("shard"),
        P("shard", None),
        P("shard"),
    )
    out_specs = (
        P(("shard", "rep"), "seq", None),
        P(("shard", "rep"), "seq", None),
        P("shard"),
        P("shard"),
        P("shard", None),
        P("shard"),
        P("shard"),
        P("shard", None),
        P("shard"),
        P("shard"),
        P("shard"),
        P("shard", None),
        P("shard"),
        P("shard", None),
        P("shard"),
    )
    return jax.shard_map(body, mesh=mesh, in_specs=in_specs, out_specs=out_specs, check_vma=False)
```
